32 devices in a mesh: batch: 8 (over y, x, core), tensor: 4 (over z).
Axes of the slice: x: 2, y: 2, z: 4, core: 2. Of those that a mesh axis runs over, the one named last changes fastest.
Arguments:
- slot_states: bfloat16 [960, 32, 768], P('tensor', 'batch'), may hold values from -6 to 6
- pass_counts: int32 [32], P('batch'), may hold values from 2 to 5
- w_qkv: bfloat16 [768, 3, 768], P(None, None, 'tensor'), may hold values from -0.21875 to 0.21875
- q_bias: bfloat16 [768], P('tensor'), may hold values from -3 to 3
- v_bias: bfloat16 [768], P('tensor'), may hold values from -0.29882812 to 0.29882812
- w_out: bfloat16 [768, 768], P('tensor'), may hold values from -1.75 to 1.75
- out_bias: bfloat16 [768], replicated, may hold values from -3 to 3
- w_up: bfloat16 [768, 3072], P(None, 'tensor'), may hold values from -0.21875 to 0.21875
- up_bias: bfloat16 [3072], P('tensor'), may hold values from -3 to 3
- w_down: bfloat16 [3072, 768], P('tensor'), may hold values from -0.109375 to 0.109375
- down_bias: bfloat16 [768], replicated, may hold values from -3 to 3
- ln1_gain: bfloat16 [768], replicated, may hold values from 0.099609375 to 1.8984375
- ln1_bias: bfloat16 [768], replicated, may hold values from -2 to 2
- ln2_gain: bfloat16 [768], replicated, may hold values from 0.099609375 to 1.8984375
- ln2_bias: bfloat16 [768], replicated, may hold values from -2 to 2
- pass_table: bfloat16 [5, 768], replicated, may hold values from -5 to 5
- cotangent: bfloat16 [960, 32, 768], P('tensor', 'batch'), may hold values from -6 to 6
Outputs:
- layer_out: bfloat16 [960, 32, 768], P('tensor', 'batch')
- grad_states: bfloat16 [960, 32, 768], P('tensor', 'batch')
- grad_qkv: float32 [768, 3, 768], P(None, None, 'tensor')
- grad_q_bias: float32 [768], P('tensor')
- grad_v_bias: float32 [768], P('tensor')
- grad_out: float32 [768, 768], P('tensor')
- grad_out_bias: float32 [768], replicated
- grad_up: float32 [768, 3072], P(None, 'tensor')
- grad_up_bias: float32 [3072], P('tensor')
- grad_down: float32 [3072, 768], P('tensor')
- grad_down_bias: float32 [768], replicated
- grad_ln1_gain: float32 [768], replicated
- grad_ln1_bias: float32 [768], replicated
- grad_ln2_gain: float32 [768], replicated
- grad_ln2_bias: float32 [768], replicated
- grad_pass: float32 [5, 768], replicated
The draws below stay inside these ranges and needn't reach their ends.
All inputs are finite; a program needn't handle non-finite values.
Results may differ from the reference program's by a relative error of at most 0.02.
Values may be sent and summed in bfloat16 or wider, within the bound.
No kernel may reach another device: no remote copies, remote signals or barrier semaphores. Data moves between devices by JAX's collectives and lax.ppermute only.
A program may use at most 256 MiB of HBM per device.

```python
import jax
import jax.numpy as jnp
from jax import lax

D = 768
HEADS = 12
HEAD_DIM = 64
FF = 3072
PASSES = 5
LEN = 192
SLOTS = 960
SEQS = 32


def plant(drawn, stream_key, least, high):
    shape = drawn.shape
    index_at = [jax.random.randint(jax.random.fold_in(stream_key, axis), (), 0, shape[axis]) for axis in range(len(shape))]
    drawn = drawn.at[tuple(index_at)].set(least)
    longest = shape.index(max(shape))
    index_at[longest] = (index_at[longest] + 1) % shape[longest]
    return drawn.at[tuple(index_at)].set(high)


def block_levels(key, shape, cuts, least, high):
    level, own = 1.0, jax.random.fold_in(key, 6)
    for axis_at, shards_of in cuts:
        draws = jnp.exp(jax.random.uniform(jax.random.fold_in(own, axis_at), (shards_of,), jnp.float32, least / len(cuts), high / len(cuts)))
        level = level * jnp.repeat(draws, shape[axis_at] // shards_of).reshape([-1 if axis == axis_at else 1 for axis in range(len(shape))])
    return level


def noise(stream_key, dims, deviation, bound, cuts=(), kind=jnp.bfloat16):
    values = deviation * jax.random.normal(stream_key, dims, jnp.float32)
    if cuts:
        values = values * block_levels(stream_key, dims, cuts, -0.22, 0.18)
    return jnp.clip(values, -bound, bound).astype(kind)


def setup_inputs(seed: int = 0) -> dict:
    seeds = jax.random.split(jax.random.key(seed), 18)
    slot_states = noise(seeds[0], (SLOTS, SEQS, D), 1.0, 6.0, ((0, 4), (1, 8)))
    pass_counts = plant(jax.random.randint(seeds[1], (SEQS,), 2, 6), jax.random.fold_in(seeds[1], 1), 2, 5).astype(jnp.int32)
    w_qkv = noise(seeds[2], (D, 3, D), D ** -0.5, 0.21875, ((2, 4),))
    q_bias = noise(seeds[3], (D,), 0.5, 3.0, ((0, 4),))
    v_bias = noise(seeds[4], (D,), 0.05, 0.29882812, ((0, 4),))
    w_out = noise(seeds[5], (D, D), (D // 64) ** -0.5, 1.75, ((0, 4),))
    out_bias = noise(seeds[6], (D,), 0.5, 3.0)
    w_up = noise(seeds[7], (D, FF), D ** -0.5, 0.21875, ((1, 4),))
    up_bias = noise(seeds[8], (FF,), 0.5, 3.0, ((0, 4),))
    w_down = noise(seeds[9], (FF, D), FF ** -0.5, 0.109375, ((0, 4),))
    down_bias = noise(seeds[10], (D,), 0.5, 3.0)
    ln1_gain = jnp.clip(1.0 + 0.18 * jax.random.normal(seeds[11], (D,), jnp.float32), 0.099609375, 1.8984375).astype(jnp.bfloat16)
    ln1_bias = noise(seeds[12], (D,), 0.3, 2.0)
    ln2_gain = jnp.clip(1.0 + 0.18 * jax.random.normal(seeds[13], (D,), jnp.float32), 0.099609375, 1.8984375).astype(jnp.bfloat16)
    ln2_bias = noise(seeds[14], (D,), 0.3, 2.0)
    pass_table = noise(seeds[15], (PASSES, D), 1.0, 5.0)
    cotangent = noise(seeds[16], (SLOTS, SEQS, D), 1.0, 6.0, ((0, 4), (1, 8)))
    return {"slot_states": slot_states, "pass_counts": pass_counts, "w_qkv": w_qkv, "q_bias": q_bias, "v_bias": v_bias, "w_out": w_out, "out_bias": out_bias, "w_up": w_up, "up_bias": up_bias, "w_down": w_down, "down_bias": down_bias, "ln1_gain": ln1_gain, "ln1_bias": ln1_bias, "ln2_gain": ln2_gain, "ln2_bias": ln2_bias, "pass_table": pass_table, "cotangent": cotangent}


@jax.custom_vjp
def low(v):
    return lax.optimization_barrier(v.astype(jnp.bfloat16)).astype(jnp.float32)

@jax.custom_vjp
def low_back(v):
    return v

def low_keep(v):
    return (low(v), None)

def low_pass(kept, grad):
    return (grad,)

def back_keep(v):
    return (v, None)

def back_low(kept, grad):
    return (low(grad),)
low.defvjp(low_keep, low_pass)
low_back.defvjp(back_keep, back_low)
HIGHEST = lax.Precision.HIGHEST
EPSILON = 1e-05
MASKED = -1e+30

def norm_rows(values, gain, shift):
    center = values - lax.optimization_barrier(jnp.mean(values, axis=-1, keepdims=True))
    spread = lax.optimization_barrier(jnp.mean(center * center, axis=-1, keepdims=True))
    return center * lax.rsqrt(spread + EPSILON) * gain + shift

def one_sequence(params, states, count):
    w_qkv, q_bias, v_bias, w_out, out_bias, w_up, up_bias, w_down, down_bias, ln1_gain, ln1_bias, ln2_gain, ln2_bias, pass_table = params
    slots = states.shape[0]
    index = jnp.arange(slots, dtype=jnp.int32)
    passes = index % count
    live = index < count * LEN
    onehot = (passes[:, None] == jnp.arange(PASSES, dtype=jnp.int32)[None, :]).astype(jnp.float32)
    hidden = states + jnp.dot(onehot, pass_table, precision=HIGHEST)
    first = low(norm_rows(hidden, ln1_gain, ln1_bias))
    projected = jnp.dot(first, w_qkv.reshape(D, 3 * D), precision=HIGHEST).reshape(slots, 3, HEADS, HEAD_DIM)
    query = low(low_back(projected[:, 0] + q_bias.reshape(HEADS, HEAD_DIM)))
    keys = low(low_back(projected[:, 1]))
    values = low(low_back(projected[:, 2] + v_bias.reshape(HEADS, HEAD_DIM)))
    scale = 1.0 / HEAD_DIM ** 0.5
    scores = low_back(jnp.einsum('qhd,khd->hqk', query, keys, precision=HIGHEST) * scale)
    allowed = (index[None, :] <= index[:, None]) & live[None, :]
    scores = jnp.where(allowed[None], scores, MASKED)
    peak = lax.optimization_barrier(jnp.max(scores, axis=-1, keepdims=True))
    powers = jnp.exp(scores - peak)
    weights = low(powers / lax.optimization_barrier(jnp.sum(powers, axis=-1, keepdims=True)))
    mixed = jnp.einsum('hqk,khd->qhd', weights, values, precision=HIGHEST)
    mixed = low(low_back(mixed)).reshape(slots, D)
    after = hidden + low_back(jnp.dot(mixed, w_out, precision=HIGHEST)) + out_bias
    second = low(norm_rows(after, ln2_gain, ln2_bias))
    pre_act = low_back(jnp.dot(second, w_up, precision=HIGHEST) + up_bias)
    activated = low(jax.nn.gelu(pre_act, approximate=True))
    result = after + low_back(jnp.dot(activated, w_down, precision=HIGHEST)) + down_bias
    return jnp.where(live[:, None], result, 0.0)

def reference(slot_states, pass_counts, w_qkv, q_bias, v_bias, w_out, out_bias, w_up, up_bias, w_down, down_bias, ln1_gain, ln1_bias, ln2_gain, ln2_bias, pass_table, cotangent):
    params = tuple((p.astype(jnp.float32) for p in (w_qkv, q_bias, v_bias, w_out, out_bias, w_up, up_bias, w_down, down_bias, ln1_gain, ln1_bias, ln2_gain, ln2_bias, pass_table)))
    states = jnp.moveaxis(slot_states.astype(jnp.float32), 1, 0)

    def forward(params, states):

        def step(item):
            return jax.checkpoint(one_sequence)(params, item[0], item[1])
        return lax.map(step, (states, pass_counts))
    outputs, pull = jax.vjp(forward, params, states)
    grads, grad_in = pull(jnp.moveaxis(cotangent.astype(jnp.float32), 1, 0))
    layer_out = jnp.moveaxis(outputs, 0, 1).astype(jnp.bfloat16)
    grad_states = jnp.moveaxis(grad_in, 0, 1).astype(jnp.bfloat16)
    return (layer_out, grad_states, grads[0], grads[1], grads[2], grads[3], grads[4], grads[5], grads[6], grads[7], grads[8], grads[9], grads[10], grads[11], grads[12], grads[13])
```

```python
import functools
import math

import jax
import jax.numpy as jnp
from jax import lax
from jax.experimental import pallas as pl
from jax.experimental.pallas import tpu as pltpu
from jax.sharding import PartitionSpec as P

HEAD_DIM = 64
PASSES = 5
LEN = 192
EPSILON = 1e-05
MASKED = -1e30
QUERY_TILE = 256
LANES = 128
F32 = jnp.float32
BF16 = jnp.bfloat16


def tiles_of(slots):
    return [(q0, min(q0 + QUERY_TILE, slots)) for q0 in range(0, slots, QUERY_TILE)]


def dot_nt(a, b):
    return lax.dot_general(a, b, (((1,), (1,)), ((), ())), preferred_element_type=F32)


def dot_nn(a, b):
    return lax.dot_general(a, b, (((1,), (0,)), ((), ())), preferred_element_type=F32)


def dot_tn(a, b):
    return lax.dot_general(a, b, (((0,), (0,)), ((), ())), preferred_element_type=F32)


def half_lanes(values, half):
    lane = lax.broadcasted_iota(jnp.int32, (1, LANES), 1)
    return jnp.where((lane // HEAD_DIM) == half, values, jnp.zeros_like(values))


def diagonal_mask(q0, rows, live):
    key = lax.broadcasted_iota(jnp.int32, (rows, rows), 0)
    query = lax.broadcasted_iota(jnp.int32, (rows, rows), 1)
    return (key <= query) & (key + q0 < live)


def attend_kernel(live_ref, q_ref, k_ref, v_ref, o_ref, lse_ref, vt_ref):
    slots = q_ref.shape[0]
    live = live_ref[0]
    vt_ref[...] = v_ref[...].T
    for q0, q1 in tiles_of(slots):
        rows = q1 - q0

        @pl.when(q0 >= live)
        def _():
            o_ref[q0:q1, :] = jnp.zeros((rows, LANES), BF16)
            lse_ref[0, :, q0:q1] = jnp.zeros((2, rows), F32)

        @pl.when(q0 < live)
        def _():
            query = q_ref[q0:q1, :] * jnp.asarray(1.0 / math.sqrt(HEAD_DIM), BF16)
            allowed = diagonal_mask(q0, rows, live)
            outs = []
            for half in range(2):
                one = half_lanes(query, half)
                last = dot_nt(k_ref[q0:q1, :], one)
                last = jnp.where(allowed, last, MASKED)
                peak = jnp.max(last, axis=0, keepdims=True)
                if q0:
                    early = dot_nt(k_ref[0:q0, :], one)
                    peak = jnp.maximum(peak, jnp.max(early, axis=0, keepdims=True))
                last = jnp.exp(last - peak)
                total = jnp.sum(last, axis=0, keepdims=True)
                lanes = slice(half * HEAD_DIM, (half + 1) * HEAD_DIM)
                if q0:
                    early = jnp.exp(early - peak)
                    total = total + jnp.sum(early, axis=0, keepdims=True)
                inverse = 1.0 / total
                out = dot_nn(vt_ref[lanes, q0:q1], (last * inverse).astype(BF16))
                if q0:
                    out = out + dot_nn(vt_ref[lanes, 0:q0], (early * inverse).astype(BF16))
                outs.append(out)
                lse_ref[0, half : half + 1, q0:q1] = peak + jnp.log(total)
            o_ref[q0:q1, :] = jnp.concatenate(outs, axis=0).T.astype(BF16)


def attend_back_kernel(
    live_ref, q_ref, k_ref, v_ref, o_ref, g_ref, lse_ref, dq_ref, dk_ref, dv_ref, kt_ref, dk_sum, dv_sum
):
    slots = q_ref.shape[0]
    live = live_ref[0]
    kt_ref[...] = k_ref[...].T
    dk_sum[...] = jnp.zeros_like(dk_sum)
    dv_sum[...] = jnp.zeros_like(dv_sum)
    scale = 1.0 / math.sqrt(HEAD_DIM)
    for q0, q1 in tiles_of(slots):
        rows = q1 - q0

        @pl.when(q0 >= live)
        def _():
            dq_ref[q0:q1, :] = jnp.zeros((rows, LANES), BF16)

        @pl.when(q0 < live)
        def _():
            query = q_ref[q0:q1, :] * jnp.asarray(scale, BF16)
            grad = g_ref[q0:q1, :]
            allowed = diagonal_mask(q0, rows, live)
            both = (grad.astype(F32) * o_ref[q0:q1, :].astype(F32)).T
            parts = []
            for half in range(2):
                lanes = slice(half * HEAD_DIM, (half + 1) * HEAD_DIM)
                one = half_lanes(query, half)
                grad_one = half_lanes(grad, half)
                lse = lse_ref[0, half : half + 1, q0:q1]
                inner = jnp.sum(both[lanes, :], axis=0, keepdims=True)
                turned = None
                for start, stop in ([(0, q0)] if q0 else []) + [(q0, q1)]:
                    scores = dot_nt(k_ref[start:stop, :], one)
                    probs = jnp.exp(scores - lse)
                    if start == q0:
                        probs = jnp.where(allowed, probs, 0.0)
                    grad_weights = dot_nt(v_ref[start:stop, :], grad_one)
                    grad_scores = (probs * (grad_weights - inner)).astype(BF16)
                    dk_sum[start:stop, :] += dot_nn(grad_scores, one)
                    dv_sum[start:stop, :] += dot_nn(probs.astype(BF16), grad_one)
                    piece = dot_nn(kt_ref[lanes, start:stop], grad_scores)
                    turned = piece if turned is None else turned + piece
                parts.append(turned)
            dq_ref[q0:q1, :] = (jnp.concatenate(parts, axis=0).T * scale).astype(BF16)

    dk_ref[...] = dk_sum[...].astype(BF16)
    dv_ref[...] = dv_sum[...].astype(BF16)


def pair_spec(slots):
    return pl.BlockSpec((slots, LANES), lambda p, live: (0, p))


def attend(live, query, keys, values):
    slots, width = query.shape
    pairs = width // LANES
    spec = pair_spec(slots)
    lse_spec = pl.BlockSpec((1, 2, slots), lambda p, live: (p, 0, 0))
    flops = 2 * 2 * slots * slots * width
    return pl.pallas_call(
        attend_kernel,
        out_shape=(
            jax.ShapeDtypeStruct((slots, width), BF16),
            jax.ShapeDtypeStruct((pairs, 2, slots), F32),
        ),
        grid_spec=pltpu.PrefetchScalarGridSpec(
            num_scalar_prefetch=1,
            grid=(pairs,),
            in_specs=[spec, spec, spec],
            out_specs=(spec, lse_spec),
            scratch_shapes=[pltpu.VMEM((LANES, slots), BF16)],
        ),
        cost_estimate=pl.CostEstimate(
            flops=flops, transcendentals=slots * slots * width // HEAD_DIM, bytes_accessed=8 * slots * width
        ),
        name="attend",
    )(live, query, keys, values)


def attend_back(live, query, keys, values, mixed, grad_mixed, lse):
    slots, width = query.shape
    pairs = width // LANES
    spec = pair_spec(slots)
    lse_spec = pl.BlockSpec((1, 2, slots), lambda p, live: (p, 0, 0))
    flops = 5 * 2 * slots * slots * width
    shape = jax.ShapeDtypeStruct((slots, width), BF16)
    return pl.pallas_call(
        attend_back_kernel,
        out_shape=(shape, shape, shape),
        grid_spec=pltpu.PrefetchScalarGridSpec(
            num_scalar_prefetch=1,
            grid=(pairs,),
            in_specs=[spec, spec, spec, spec, spec, lse_spec],
            out_specs=(spec, spec, spec),
            scratch_shapes=[
                pltpu.VMEM((LANES, slots), BF16),
                pltpu.VMEM((slots, LANES), F32),
                pltpu.VMEM((slots, LANES), F32),
            ],
        ),
        cost_estimate=pl.CostEstimate(
            flops=flops, transcendentals=slots * slots * width // HEAD_DIM, bytes_accessed=16 * slots * width
        ),
        name="attend_back",
    )(live, query, keys, values, mixed, grad_mixed, lse)


def ring_pairs(size, shift):
    return [(source, (source + shift) % size) for source in range(size)]


def to_sequence(block):
    size = lax.axis_size("tensor")
    me = lax.axis_index("tensor")
    rows, seqs, width = block.shape
    block = block.transpose(1, 0, 2)
    out = jnp.zeros((size * rows, width), block.dtype)
    for shift in range(size):
        piece = lax.dynamic_index_in_dim(block, (me + shift) % size, 0, keepdims=False)
        if shift:
            piece = lax.ppermute(piece, "tensor", ring_pairs(size, shift))
        out = lax.dynamic_update_slice(out, piece, (((me - shift) % size) * rows, 0))
    return out


def to_slots(values):
    size = lax.axis_size("tensor")
    me = lax.axis_index("tensor")
    slots, width = values.shape
    rows = slots // size
    out = jnp.zeros((size, rows, width), values.dtype)
    for shift in range(size):
        piece = lax.dynamic_slice(values, (((me + shift) % size) * rows, 0), (rows, width))
        if shift:
            piece = lax.ppermute(piece, "tensor", ring_pairs(size, shift))
        out = lax.dynamic_update_slice(out, piece[None], ((me - shift) % size, 0, 0))
    return out.transpose(1, 0, 2)


def share(rows):
    size = lax.axis_size("batch")
    each = rows.shape[0] // size
    return lax.dynamic_slice(rows, (lax.axis_index("batch") * each, 0), (each, rows.shape[1]))


def norm_parts(values):
    mean = jnp.mean(values, axis=-1, keepdims=True)
    center = values - mean
    spread = jnp.mean(center * center, axis=-1, keepdims=True)
    inverse = lax.rsqrt(spread + EPSILON)
    return center * inverse, inverse


def norm_back(grad, xhat, inverse, gain):
    scaled = grad * gain
    first = jnp.mean(scaled, axis=-1, keepdims=True)
    second = jnp.mean(scaled * xhat, axis=-1, keepdims=True)
    return inverse * (scaled - first - xhat * second)


def gelu_parts(values):
    outer = math.sqrt(2.0 / math.pi)
    inside = jnp.tanh(outer * (values + 0.044715 * values * values * values))
    act = 0.5 * values * (1.0 + inside)
    slope = 0.5 * (1.0 + inside) + 0.5 * values * (1.0 - inside * inside) * outer * (
        1.0 + 3.0 * 0.044715 * values * values
    )
    return act, slope


def per_device(
    slot_states,
    pass_counts,
    w_qkv,
    q_bias,
    v_bias,
    w_out,
    out_bias,
    w_up,
    up_bias,
    w_down,
    down_bias,
    ln1_gain,
    ln1_bias,
    ln2_gain,
    ln2_bias,
    pass_table,
    cotangent,
):
    groups = lax.axis_size("tensor")
    spread = lax.axis_size("batch")
    me = lax.axis_index("tensor")
    rows, seqs, width = slot_states.shape
    slots = rows * groups
    hidden_here = w_up.shape[1]
    hidden_units = hidden_here * groups
    assert seqs == groups

    gain_one, shift_one = ln1_gain.astype(F32), ln1_bias.astype(F32)
    gain_two, shift_two = ln2_gain.astype(F32), ln2_bias.astype(F32)
    table = pass_table.astype(F32)

    qkv_rows = w_qkv.transpose(1, 2, 0)
    every = ("tensor", "batch")
    gathered_qkv = lax.all_gather(
        jnp.concatenate([share(qkv_rows[part]) for part in range(3)], axis=0)[None], every, axis=0, tiled=True
    )
    each = width // (groups * spread)
    gathered_qkv = gathered_qkv.reshape(groups * spread, 3, each, width)
    matrix_q, matrix_k, matrix_v = (gathered_qkv[:, part].reshape(width, width) for part in range(3))
    matrix_out = lax.all_gather(share(w_out), every, axis=0, tiled=True)
    mixed_order = ("batch", "tensor")
    matrix_up = lax.all_gather(share(w_up.T), mixed_order, axis=0, tiled=True)
    matrix_down = lax.all_gather(share(w_down), mixed_order, axis=0, tiled=True)
    bias_row = jnp.concatenate([q_bias, v_bias, up_bias]).astype(BF16)
    bias_rows = lax.all_gather(bias_row, "tensor", axis=0)
    here = q_bias.shape[0]
    bias_query = bias_rows[:, :here].reshape(1, width).astype(F32)
    bias_value = bias_rows[:, here : 2 * here].reshape(1, width).astype(F32)
    bias_up = bias_rows[:, 2 * here :].reshape(groups, spread, hidden_here // spread)
    bias_up = bias_up.transpose(1, 0, 2).reshape(1, hidden_units).astype(F32)

    states = to_sequence(slot_states).astype(F32)
    cot = to_sequence(cotangent)
    count = lax.dynamic_index_in_dim(pass_counts, me, 0, keepdims=False)
    index = jnp.arange(slots, dtype=jnp.int32)
    passes = (index % count)[:, None]
    live_count = count * LEN
    live = (index < live_count)[:, None]
    live_arg = live_count.reshape(1).astype(jnp.int32)
    added = jnp.zeros((slots, width), F32)
    for number in range(PASSES):
        added = jnp.where(passes == number, table[number][None, :], added)
    hidden = states + added

    xhat_one, inverse_one = norm_parts(hidden)
    n1 = (xhat_one * gain_one + shift_one).astype(BF16)
    query = (dot_nt(n1, matrix_q) + bias_query).astype(BF16)
    keys = dot_nt(n1, matrix_k).astype(BF16)
    values = (dot_nt(n1, matrix_v) + bias_value).astype(BF16)
    mixed, lse = attend(live_arg, query, keys, values)
    after = hidden + dot_nn(mixed, matrix_out) + out_bias.astype(F32)
    xhat_two, inverse_two = norm_parts(after)
    n2 = (xhat_two * gain_two + shift_two).astype(BF16)
    pre_act = dot_nt(n2, matrix_up) + bias_up
    act, slope = gelu_parts(pre_act)
    act = act.astype(BF16)
    result = after + dot_nn(act, matrix_down) + down_bias.astype(F32)
    layer_out = jnp.where(live, result, 0.0).astype(BF16)
    layer_part = to_slots(layer_out)

    grad_m = jnp.where(live, cot, jnp.zeros_like(cot))
    grad_y = grad_m.astype(F32)
    grad_down = dot_tn(act, grad_m).astype(BF16)
    grad_act = dot_nt(grad_m, matrix_down)
    grad_u = (grad_act * slope).astype(BF16)
    grad_up = dot_tn(grad_u, n2).astype(BF16)
    grad_n2 = dot_nn(grad_u, matrix_up)
    grad_a = grad_y + norm_back(grad_n2, xhat_two, inverse_two, gain_two)
    grad_att = grad_a.astype(BF16)
    grad_out = dot_tn(mixed, grad_att).astype(BF16)
    grad_mixed = dot_nt(grad_att, matrix_out).astype(BF16)
    grad_q, grad_k, grad_v = attend_back(live_arg, query, keys, values, mixed, grad_mixed, lse)
    grad_wq = dot_tn(grad_q, n1).astype(BF16)
    grad_wk = dot_tn(grad_k, n1).astype(BF16)
    grad_wv = dot_tn(grad_v, n1).astype(BF16)
    grad_n1 = dot_nn(grad_q, matrix_q) + dot_nn(grad_k, matrix_k) + dot_nn(grad_v, matrix_v)
    grad_h = grad_a + norm_back(grad_n1, xhat_one, inverse_one, gain_one)
    grad_part = to_slots(grad_h.astype(BF16))

    def reduce_mixed(value):
        value = lax.psum_scatter(value, "batch", scatter_dimension=0, tiled=True)
        value = lax.psum_scatter(value, "tensor", scatter_dimension=0, tiled=True)
        return lax.all_gather(value, "batch", axis=0, tiled=True).astype(F32)

    def reduce_plain(value):
        value = value.reshape(groups, -1, width)
        value = lax.psum_scatter(value, "batch", scatter_dimension=1, tiled=True)
        value = lax.psum_scatter(value, "tensor", scatter_dimension=0, tiled=True)
        return lax.all_gather(value[0], "batch", axis=0, tiled=True).astype(F32)

    out_down = reduce_mixed(grad_down)
    out_up = reduce_mixed(grad_up).T
    out_out = reduce_plain(grad_out)
    out_qkv = jnp.stack([reduce_plain(value) for value in (grad_wq, grad_wk, grad_wv)], axis=0).transpose(2, 0, 1)

    def total(value):
        return jnp.sum(value.astype(F32), axis=0, keepdims=True)

    grad_pass = jnp.concatenate(
        [total(jnp.where(passes == number, grad_h, 0.0)) for number in range(PASSES)], axis=0
    )
    grad_bias_up = total(grad_u).reshape(spread, groups, hidden_here // spread)
    grad_bias_up = grad_bias_up.transpose(1, 0, 2).reshape(groups, width)
    small = jnp.concatenate(
        [
            total(grad_n1 * xhat_one),
            total(grad_n1),
            total(grad_n2 * xhat_two),
            total(grad_n2),
            total(grad_a),
            total(grad_y),
            grad_pass,
            total(grad_q),
            total(grad_v),
            grad_bias_up,
        ],
        axis=0,
    )
    small = lax.psum(small, ("batch", "tensor"))
    lead = 6 + PASSES
    mine = lax.dynamic_slice_in_dim(small[lead : lead + 2], me * here, here, axis=1)
    return (
        layer_part,
        grad_part,
        out_qkv,
        mine[0],
        mine[1],
        out_out,
        small[4],
        out_up,
        lax.dynamic_index_in_dim(small[lead + 2 :], me, 0, keepdims=False),
        out_down,
        small[5],
        small[0],
        small[1],
        small[2],
        small[3],
        small[6:lead],
    )


def solution(mesh):
    in_specs = (
        P("tensor", "batch", None),
        P("batch"),
        P(None, None, "tensor"),
        P("tensor"),
        P("tensor"),
        P("tensor", None),
        P(),
        P(None, "tensor"),
        P("tensor"),
        P("tensor", None),
        P(),
        P(),
        P(),
        P(),
        P(),
        P(),
        P("tensor", "batch", None),
    )
    out_specs = (
        P("tensor", "batch", None),
        P("tensor", "batch", None),
        P(None, None, "tensor"),
        P("tensor"),
        P("tensor"),
        P("tensor", None),
        P(),
        P(None, "tensor"),
        P("tensor"),
        P("tensor", None),
        P(),
        P(),
        P(),
        P(),
        P(),
        P(),
    )
    return jax.shard_map(
        per_device, mesh=mesh, in_specs=in_specs, out_specs=out_specs, check_vma=False
    )
```

```python
import functools
import math

import jax
import jax.numpy as jnp
from jax import lax
from jax.experimental import pallas as pl
from jax.experimental.pallas import tpu as pltpu
from jax.sharding import PartitionSpec as P

HEAD_DIM = 64
PASSES = 5
LEN = 192
EPSILON = 1e-05
MASKED = -1e30
QUERY_TILE = 256
LANES = 128
F32 = jnp.float32
BF16 = jnp.bfloat16


def tiles_of(slots):
    return [(q0, min(q0 + QUERY_TILE, slots)) for q0 in range(0, slots, QUERY_TILE)]


def dot_nt(a, b):
    return lax.dot_general(a, b, (((1,), (1,)), ((), ())), preferred_element_type=F32)


def dot_nn(a, b):
    return lax.dot_general(a, b, (((1,), (0,)), ((), ())), preferred_element_type=F32)


def dot_tn(a, b):
    return lax.dot_general(a, b, (((0,), (0,)), ((), ())), preferred_element_type=F32)


def half_lanes(values, half):
    lane = lax.broadcasted_iota(jnp.int32, (1, LANES), 1)
    return jnp.where((lane // HEAD_DIM) == half, values, jnp.zeros_like(values))


def diagonal_mask(q0, rows, live):
    key = lax.broadcasted_iota(jnp.int32, (rows, rows), 0)
    query = lax.broadcasted_iota(jnp.int32, (rows, rows), 1)
    return (key <= query) & (key + q0 < live)


def attend_kernel(live_ref, q_ref, k_ref, v_ref, o_ref, lse_ref, vt_ref):
    slots = q_ref.shape[0]
    live = live_ref[0]
    vt_ref[...] = v_ref[...].T
    for q0, q1 in tiles_of(slots):
        rows = q1 - q0

        @pl.when(q0 >= live)
        def _():
            o_ref[q0:q1, :] = jnp.zeros((rows, LANES), BF16)
            lse_ref[0, :, q0:q1] = jnp.zeros((2, rows), F32)

        @pl.when(q0 < live)
        def _():
            query = q_ref[q0:q1, :] * jnp.asarray(1.0 / math.sqrt(HEAD_DIM), BF16)
            allowed = diagonal_mask(q0, rows, live)
            outs = []
            for half in range(2):
                one = half_lanes(query, half)
                last = dot_nt(k_ref[q0:q1, :], one)
                last = jnp.where(allowed, last, MASKED)
                peak = jnp.max(last, axis=0, keepdims=True)
                if q0:
                    early = dot_nt(k_ref[0:q0, :], one)
                    peak = jnp.maximum(peak, jnp.max(early, axis=0, keepdims=True))
                last = jnp.exp(last - peak)
                total = jnp.sum(last, axis=0, keepdims=True)
                lanes = slice(half * HEAD_DIM, (half + 1) * HEAD_DIM)
                if q0:
                    early = jnp.exp(early - peak)
                    total = total + jnp.sum(early, axis=0, keepdims=True)
                inverse = 1.0 / total
                out = dot_nn(vt_ref[lanes, q0:q1], (last * inverse).astype(BF16))
                if q0:
                    out = out + dot_nn(vt_ref[lanes, 0:q0], (early * inverse).astype(BF16))
                outs.append(out)
                lse_ref[0, half : half + 1, q0:q1] = peak + jnp.log(total)
            o_ref[q0:q1, :] = jnp.concatenate(outs, axis=0).T.astype(BF16)


def attend_back_kernel(
    live_ref, q_ref, k_ref, v_ref, o_ref, g_ref, lse_ref, dq_ref, dk_ref, dv_ref, kt_ref, dk_sum, dv_sum
):
    slots = q_ref.shape[0]
    live = live_ref[0]
    kt_ref[...] = k_ref[...].T
    dk_sum[...] = jnp.zeros_like(dk_sum)
    dv_sum[...] = jnp.zeros_like(dv_sum)
    scale = 1.0 / math.sqrt(HEAD_DIM)
    for q0, q1 in tiles_of(slots):
        rows = q1 - q0

        @pl.when(q0 >= live)
        def _():
            dq_ref[q0:q1, :] = jnp.zeros((rows, LANES), BF16)

        @pl.when(q0 < live)
        def _():
            query = q_ref[q0:q1, :] * jnp.asarray(scale, BF16)
            grad = g_ref[q0:q1, :]
            allowed = diagonal_mask(q0, rows, live)
            both = (grad.astype(F32) * o_ref[q0:q1, :].astype(F32)).T
            parts = []
            for half in range(2):
                lanes = slice(half * HEAD_DIM, (half + 1) * HEAD_DIM)
                one = half_lanes(query, half)
                grad_one = half_lanes(grad, half)
                lse = lse_ref[0, half : half + 1, q0:q1]
                inner = jnp.sum(both[lanes, :], axis=0, keepdims=True)
                turned = None
                for start, stop in ([(0, q0)] if q0 else []) + [(q0, q1)]:
                    scores = dot_nt(k_ref[start:stop, :], one)
                    probs = jnp.exp(scores - lse)
                    if start == q0:
                        probs = jnp.where(allowed, probs, 0.0)
                    grad_weights = dot_nt(v_ref[start:stop, :], grad_one)
                    grad_scores = (probs * (grad_weights - inner)).astype(BF16)
                    dk_sum[start:stop, :] += dot_nn(grad_scores, one)
                    dv_sum[start:stop, :] += dot_nn(probs.astype(BF16), grad_one)
                    piece = dot_nn(kt_ref[lanes, start:stop], grad_scores)
                    turned = piece if turned is None else turned + piece
                parts.append(turned)
            dq_ref[q0:q1, :] = (jnp.concatenate(parts, axis=0).T * scale).astype(BF16)

    dk_ref[...] = dk_sum[...].astype(BF16)
    dv_ref[...] = dv_sum[...].astype(BF16)


def pair_spec(slots):
    return pl.BlockSpec((slots, LANES), lambda p, live: (0, p))


def attend(live, query, keys, values):
    slots, width = query.shape
    pairs = width // LANES
    spec = pair_spec(slots)
    lse_spec = pl.BlockSpec((1, 2, slots), lambda p, live: (p, 0, 0))
    flops = 2 * 2 * slots * slots * width
    return pl.pallas_call(
        attend_kernel,
        out_shape=(
            jax.ShapeDtypeStruct((slots, width), BF16),
            jax.ShapeDtypeStruct((pairs, 2, slots), F32),
        ),
        grid_spec=pltpu.PrefetchScalarGridSpec(
            num_scalar_prefetch=1,
            grid=(pairs,),
            in_specs=[spec, spec, spec],
            out_specs=(spec, lse_spec),
            scratch_shapes=[pltpu.VMEM((LANES, slots), BF16)],
        ),
        cost_estimate=pl.CostEstimate(
            flops=flops, transcendentals=slots * slots * width // HEAD_DIM, bytes_accessed=8 * slots * width
        ),
        name="attend",
    )(live, query, keys, values)


def attend_back(live, query, keys, values, mixed, grad_mixed, lse):
    slots, width = query.shape
    pairs = width // LANES
    spec = pair_spec(slots)
    lse_spec = pl.BlockSpec((1, 2, slots), lambda p, live: (p, 0, 0))
    flops = 5 * 2 * slots * slots * width
    shape = jax.ShapeDtypeStruct((slots, width), BF16)
    return pl.pallas_call(
        attend_back_kernel,
        out_shape=(shape, shape, shape),
        grid_spec=pltpu.PrefetchScalarGridSpec(
            num_scalar_prefetch=1,
            grid=(pairs,),
            in_specs=[spec, spec, spec, spec, spec, lse_spec],
            out_specs=(spec, spec, spec),
            scratch_shapes=[
                pltpu.VMEM((LANES, slots), BF16),
                pltpu.VMEM((slots, LANES), F32),
                pltpu.VMEM((slots, LANES), F32),
            ],
        ),
        cost_estimate=pl.CostEstimate(
            flops=flops, transcendentals=slots * slots * width // HEAD_DIM, bytes_accessed=16 * slots * width
        ),
        name="attend_back",
    )(live, query, keys, values, mixed, grad_mixed, lse)


def ring_pairs(size, shift):
    return [(source, (source + shift) % size) for source in range(size)]


def to_sequence(block):
    size = lax.axis_size("tensor")
    me = lax.axis_index("tensor")
    rows, seqs, width = block.shape
    block = lax.optimization_barrier(block.transpose(1, 0, 2))
    out = jnp.zeros((size * rows, width), block.dtype)
    for shift in range(size):
        piece = lax.dynamic_index_in_dim(block, (me + shift) % size, 0, keepdims=False)
        if shift:
            piece = lax.ppermute(piece, "tensor", ring_pairs(size, shift))
        out = lax.dynamic_update_slice(out, piece, (((me - shift) % size) * rows, 0))
    return out


def to_slots(values):
    size = lax.axis_size("tensor")
    me = lax.axis_index("tensor")
    slots, width = values.shape
    rows = slots // size
    out = jnp.zeros((slots, width), values.dtype)
    for shift in range(size):
        piece = lax.dynamic_slice(values, (((me + shift) % size) * rows, 0), (rows, width))
        if shift:
            piece = lax.ppermute(piece, "tensor", ring_pairs(size, shift))
        out = lax.dynamic_update_slice(out, piece, (((me - shift) % size) * rows, 0))
    return lax.optimization_barrier(out).reshape(size, rows, width).transpose(1, 0, 2)


def gather_pieces(shard):
    size = lax.axis_size("tensor")
    me = lax.axis_index("tensor")
    core = lax.axis_index("batch") % 2
    rows, width = shard.shape
    half = rows // 2
    partners = [(place, place ^ 1) for place in range(lax.axis_size("batch"))]
    mine = lax.dynamic_slice(shard, (core * half, 0), (half, width))
    out = lax.dynamic_update_slice(jnp.zeros((size * rows, width), shard.dtype), shard, (me * rows, 0))
    for shift in range(1, size):
        piece = lax.ppermute(mine, "tensor", ring_pairs(size, shift))
        other = lax.ppermute(piece, "batch", partners)
        first = ((me - shift) % size) * rows
        out = lax.dynamic_update_slice(out, piece, (first + core * half, 0))
        out = lax.dynamic_update_slice(out, other, (first + (1 - core) * half, 0))
    return out.reshape(size, rows, width)


def share(rows):
    size = lax.axis_size("batch")
    each = rows.shape[0] // size
    return lax.dynamic_slice(rows, (lax.axis_index("batch") * each, 0), (each, rows.shape[1]))


def norm_parts(values):
    mean = jnp.mean(values, axis=-1, keepdims=True)
    center = values - mean
    spread = jnp.mean(center * center, axis=-1, keepdims=True)
    inverse = lax.rsqrt(spread + EPSILON)
    return center * inverse, inverse


def norm_back(grad, xhat, inverse, gain):
    scaled = grad * gain
    first = jnp.mean(scaled, axis=-1, keepdims=True)
    second = jnp.mean(scaled * xhat, axis=-1, keepdims=True)
    return inverse * (scaled - first - xhat * second)


def gelu_parts(values):
    outer = math.sqrt(2.0 / math.pi)
    inside = jnp.tanh(outer * (values + 0.044715 * values * values * values))
    act = 0.5 * values * (1.0 + inside)
    slope = 0.5 * (1.0 + inside) + 0.5 * values * (1.0 - inside * inside) * outer * (
        1.0 + 3.0 * 0.044715 * values * values
    )
    return act, slope


def rows_in(slots):
    return [(r0, min(r0 + 240, slots)) for r0 in range(0, slots, 240)]


def mlp_kernel(
    live_ref, hid_ref, mix_ref, wo_ref, cot_ref, vec_ref, bup_ref, up_ref, down_ref,
    y_ref, ga_ref, gmix_ref, gblock_ref, gwo_ref, sums_ref, gbup_ref,
    n2_s, xhat_s, inv_s, y_s, d_s, gm_s,
):
    slots = hid_ref.shape[0]
    step = pl.program_id(0)
    live = live_ref[0]

    def live_rows(r0, r1):
        return lax.broadcasted_iota(jnp.int32, (r1 - r0, 1), 0) + r0 < live

    @pl.when(step == 0)
    def _():
        for r0, r1 in rows_in(slots):
            after = hid_ref[r0:r1, :] + dot_nn(mix_ref[r0:r1, :], wo_ref[...]) + vec_ref[0:1, :]
            xhat, inverse = norm_parts(after)
            xhat_s[r0:r1, :] = xhat
            inv_s[r0:r1, :] = inverse
            n2_s[r0:r1, :] = (xhat * vec_ref[1:2, :] + vec_ref[2:3, :]).astype(BF16)
            y_s[r0:r1, :] = after + vec_ref[3:4, :]
            cot = cot_ref[r0:r1, :]
            gm_s[r0:r1, :] = jnp.where(live_rows(r0, r1), cot, jnp.zeros_like(cot))
            d_s[r0:r1, :] = jnp.zeros((r1 - r0, d_s.shape[1]), F32)

    count, units, width = up_ref.shape
    up = up_ref[...].reshape(count * units, width)
    down = down_ref[...].reshape(count * units, width)
    n2 = n2_s[...]
    grad_m = gm_s[...]
    act, slope = gelu_parts(dot_nt(n2, up) + bup_ref[...])
    act = act.astype(BF16)
    grad_u = (dot_nt(grad_m, down) * slope).astype(BF16)
    y_s[...] += dot_nn(act, down)
    d_s[...] += dot_nn(grad_u, up)
    gblock_ref[:, 0, 0:units, :] = dot_tn(grad_u, n2).reshape(count, units, width).astype(BF16)
    gblock_ref[:, 0, units : 2 * units, :] = dot_tn(act, grad_m).reshape(count, units, width).astype(BF16)
    gbup_ref[...] = jnp.sum(grad_u.astype(F32), axis=0, keepdims=True)

    @pl.when(step == pl.num_programs(0) - 1)
    def _():
        sums = [jnp.zeros((1, width), F32)] * 4
        for r0, r1 in rows_in(slots):
            y_ref[r0:r1, :] = jnp.where(live_rows(r0, r1), y_s[r0:r1, :], 0.0).astype(BF16)
            grad_n2 = d_s[r0:r1, :]
            xhat = xhat_s[r0:r1, :]
            grad_y = gm_s[r0:r1, :].astype(F32)
            grad_a = grad_y + norm_back(grad_n2, xhat, inv_s[r0:r1, :], vec_ref[1:2, :])
            ga_ref[r0:r1, :] = grad_a
            grad_att = grad_a.astype(BF16)
            n2_s[r0:r1, :] = grad_att
            gmix_ref[r0:r1, :] = dot_nt(grad_att, wo_ref[...]).astype(BF16)
            for place, value in enumerate((grad_n2 * xhat, grad_n2, grad_a, grad_y)):
                sums[place] = sums[place] + jnp.sum(value, axis=0, keepdims=True)
        gwo_ref[...] = dot_tn(mix_ref[...], n2_s[...]).astype(BF16)
        for place in range(4):
            sums_ref[place : place + 1, :] = sums[place]
        sums_ref[4:8, :] = jnp.zeros((4, width), F32)


def mlp(live, hidden, mixed, w_out, cot, vectors, bias_up, blocks, blocks_first, spread, groups, units):
    slots, width = hidden.shape
    take = 4
    chunk = take * units
    steps = groups * spread // take
    per_group = spread // take
    one = pl.Buffered(1)

    def whole(shape):
        return pl.BlockSpec(shape, lambda c, live: (0,) * len(shape), pipeline_mode=one)

    full = whole((slots, width))
    flops = 2 * slots * width * (6 * units * groups * spread + 3 * width)
    return pl.pallas_call(
        mlp_kernel,
        out_shape=(
            jax.ShapeDtypeStruct((slots, width), BF16),
            jax.ShapeDtypeStruct((slots, width), F32),
            jax.ShapeDtypeStruct((slots, width), BF16),
            jax.ShapeDtypeStruct((spread, groups, 2 * units, width), BF16),
            jax.ShapeDtypeStruct((width, width), BF16),
            jax.ShapeDtypeStruct((8, width), F32),
            jax.ShapeDtypeStruct((1, steps * chunk), F32),
        ),
        grid_spec=pltpu.PrefetchScalarGridSpec(
            num_scalar_prefetch=1,
            grid=(steps,),
            in_specs=[
                full,
                full,
                whole((width, width)),
                full,
                whole((8, width)),
                pl.BlockSpec((1, chunk), lambda c, live: (0, c)),
                pl.BlockSpec((take, units, width), lambda c, live: (c, blocks_first, 0)),
                pl.BlockSpec((take, units, width), lambda c, live: (c, blocks_first + 1, 0)),
            ],
            out_specs=(
                full,
                full,
                full,
                pl.BlockSpec((take, 1, 2 * units, width), lambda c, live: (c % per_group, c // per_group, 0, 0)),
                whole((width, width)),
                whole((8, width)),
                pl.BlockSpec((1, chunk), lambda c, live: (0, c)),
            ),
            scratch_shapes=[
                pltpu.VMEM((slots, width), BF16),
                pltpu.VMEM((slots, width), F32),
                pltpu.VMEM((slots, 1), F32),
                pltpu.VMEM((slots, width), F32),
                pltpu.VMEM((slots, width), F32),
                pltpu.VMEM((slots, width), BF16),
            ],
        ),
        cost_estimate=pl.CostEstimate(
            flops=flops, transcendentals=slots * steps * chunk, bytes_accessed=20 * slots * width + 8 * steps * chunk * width
        ),
        name="mlp",
    )(live, hidden, mixed, w_out, cot, vectors, bias_up, blocks, blocks)


def per_device(
    slot_states,
    pass_counts,
    w_qkv,
    q_bias,
    v_bias,
    w_out,
    out_bias,
    w_up,
    up_bias,
    w_down,
    down_bias,
    ln1_gain,
    ln1_bias,
    ln2_gain,
    ln2_bias,
    pass_table,
    cotangent,
):
    groups = lax.axis_size("tensor")
    spread = lax.axis_size("batch")
    me = lax.axis_index("tensor")
    rows, seqs, width = slot_states.shape
    slots = rows * groups
    hidden_here = w_up.shape[1]
    hidden_units = hidden_here * groups
    assert seqs == groups

    gain_one, shift_one = ln1_gain.astype(F32), ln1_bias.astype(F32)
    gain_two, shift_two = ln2_gain.astype(F32), ln2_bias.astype(F32)
    table = pass_table.astype(F32)

    each = width // (groups * spread)
    units = hidden_here // spread
    here = q_bias.shape[0]
    states = to_sequence(slot_states).astype(F32)
    biases = jnp.concatenate([q_bias, v_bias, jnp.zeros((width - 2 * here,), BF16)]).reshape(1, width)
    shard = jnp.concatenate(
        [w_qkv.transpose(1, 2, 0).reshape(3 * here, width), jnp.pad(biases, ((0, 15), (0, 0)))], axis=0
    )
    shards = gather_pieces(shard)
    matrix_q, matrix_k, matrix_v = (
        shards[:, part * here : (part + 1) * here].reshape(width, width) for part in range(3)
    )
    bias_rows = shards[:, 3 * here].astype(F32)
    bias_query = bias_rows[:, :here].reshape(1, width)
    bias_value = bias_rows[:, here : 2 * here].reshape(1, width)

    bias_row = jnp.pad(up_bias.reshape(1, width), ((0, 15), (0, 0)))
    block = jnp.concatenate([share(w_up.T), share(w_down), share(w_out), bias_row], axis=0)
    blocks = lax.all_gather(block, ("tensor", "batch"), axis=0, tiled=False)
    matrix_out = blocks[:, 2 * units : 2 * units + each].reshape(width, width)
    bias_up = blocks.reshape(groups, spread, block.shape[0], width)[:, 0, 2 * units + each]
    bias_up = bias_up.reshape(1, hidden_units).astype(F32)

    count = lax.dynamic_index_in_dim(pass_counts, me, 0, keepdims=False)
    index = jnp.arange(slots, dtype=jnp.int32)
    passes = (index % count)[:, None]
    live_count = count * LEN
    live = (index < live_count)[:, None]
    live_arg = live_count.reshape(1).astype(jnp.int32)
    added = jnp.zeros((slots, width), F32)
    for number in range(PASSES):
        added = jnp.where(passes == number, table[number][None, :], added)
    hidden = states + added

    xhat_one, inverse_one = norm_parts(hidden)
    n1 = (xhat_one * gain_one + shift_one).astype(BF16)
    query = (dot_nt(n1, matrix_q) + bias_query).astype(BF16)
    keys = dot_nt(n1, matrix_k).astype(BF16)
    values = (dot_nt(n1, matrix_v) + bias_value).astype(BF16)
    query, cotangent = lax.optimization_barrier((query, cotangent))
    cot = to_sequence(cotangent)
    mixed, lse = attend(live_arg, query, keys, values)
    vectors = jnp.stack([out_bias.astype(F32), gain_two, shift_two, down_bias.astype(F32)])
    vectors = jnp.pad(vectors, ((0, 4), (0, 0)))
    regroup = units % 32 != 0
    fold, fold_units = (8, hidden_here // 8) if regroup else (spread, units)
    if regroup:
        blocks = jnp.concatenate(
            [
                blocks[:, part * units : (part + 1) * units].reshape(groups * fold, fold_units, width)
                for part in range(2)
            ],
            axis=1,
        )
    layer_out, grad_a, grad_mixed, mlp_block, grad_out, sums, grad_bias_up = mlp(
        live_arg, hidden, mixed, matrix_out, cot, vectors, bias_up, blocks, 0, fold, groups, fold_units
    )
    if regroup:
        mlp_block = mlp_block.reshape(fold, groups, 2, fold_units, width).transpose(1, 2, 0, 3, 4)
        mlp_block = mlp_block.reshape(groups, 2, spread, units, width).transpose(2, 0, 1, 3, 4)
        mlp_block = mlp_block.reshape(spread, groups, 2 * units, width)
    layer_part = to_slots(layer_out)
    grad_q, grad_k, grad_v = attend_back(live_arg, query, keys, values, mixed, grad_mixed, lse)
    grad_q, layer_part = lax.optimization_barrier((grad_q, layer_part))
    grad_wq = dot_tn(grad_q, n1).astype(BF16)
    grad_wk = dot_tn(grad_k, n1).astype(BF16)
    grad_wv = dot_tn(grad_v, n1).astype(BF16)
    grad_n1 = dot_nn(grad_q, matrix_q) + dot_nn(grad_k, matrix_k) + dot_nn(grad_v, matrix_v)
    grad_h = grad_a + norm_back(grad_n1, xhat_one, inverse_one, gain_one)
    grad_part = to_slots(grad_h.astype(BF16))

    def total(value):
        return jnp.sum(value.astype(F32), axis=0, keepdims=True)

    grad_bias_up = grad_bias_up.reshape(groups, 1, hidden_here)
    common = jnp.concatenate(
        [
            total(grad_n1 * xhat_one),
            total(grad_n1),
            sums[0:4],
        ]
        + [total(jnp.where(passes == number, grad_h, 0.0)) for number in range(PASSES)],
        axis=0,
    )
    lead = common.shape[0]
    own = jnp.concatenate(
        [
            total(grad_q).reshape(groups, 1, here),
            total(grad_v).reshape(groups, 1, here),
            jnp.zeros((groups, 1, width - 2 * here), F32),
        ],
        axis=2,
    )
    small = jnp.concatenate(
        [jnp.broadcast_to(common[None], (groups, lead, width)), own, grad_bias_up], axis=1
    )
    extra = 16
    small = jnp.pad(small, ((0, 0), (0, spread * extra - lead - 2), (0, 0)))
    small = small.reshape(groups, spread, extra, width).transpose(1, 0, 2, 3).astype(BF16)

    def spread_rows(value):
        return value.reshape(groups, spread, each, width).transpose(1, 0, 2, 3)

    attn_block = jnp.concatenate(
        [spread_rows(value) for value in (grad_wq, grad_wk, grad_wv, grad_out)] + [small], axis=2
    )
    def over_tensor(value):
        kept = lax.dynamic_index_in_dim(value, me, 0, keepdims=False).astype(F32)
        for shift in range(1, groups):
            piece = lax.dynamic_index_in_dim(value, (me + shift) % groups, 0, keepdims=False)
            kept = kept + lax.ppermute(piece, "tensor", ring_pairs(groups, shift)).astype(F32)
        return kept.astype(BF16)

    mlp_block = lax.psum_scatter(mlp_block, "batch", scatter_dimension=0, tiled=True)[0]
    attn_block, mlp_block = lax.optimization_barrier((attn_block, mlp_block))
    attn_block = lax.psum_scatter(attn_block, "batch", scatter_dimension=0, tiled=True)[0]
    mlp_piece = over_tensor(mlp_block)
    attn_piece = over_tensor(attn_block)
    whole = lax.all_gather(jnp.concatenate([attn_piece, mlp_piece], axis=0), "batch", axis=0, tiled=False)
    parts = [whole[:, part * each : (part + 1) * each].reshape(here, width).astype(F32) for part in range(4)]
    small = whole[:, 4 * each : 4 * each + extra].reshape(spread * extra, width).astype(F32)
    base = 4 * each + extra
    out_up = whole[:, base : base + units].reshape(hidden_here, width).astype(F32).T
    out_down = whole[:, base + units :].reshape(hidden_here, width).astype(F32)
    out_qkv = jnp.stack(parts[:3], axis=0).transpose(2, 0, 1)
    return (
        layer_part,
        grad_part,
        out_qkv,
        small[lead, :here],
        small[lead, here : 2 * here],
        parts[3],
        small[4],
        out_up,
        small[lead + 1],
        out_down,
        small[5],
        small[0],
        small[1],
        small[2],
        small[3],
        small[6:lead],
    )


def solution(mesh):
    in_specs = (
        P("tensor", "batch", None),
        P("batch"),
        P(None, None, "tensor"),
        P("tensor"),
        P("tensor"),
        P("tensor", None),
        P(),
        P(None, "tensor"),
        P("tensor"),
        P("tensor", None),
        P(),
        P(),
        P(),
        P(),
        P(),
        P(),
        P("tensor", "batch", None),
    )
    out_specs = (
        P("tensor", "batch", None),
        P("tensor", "batch", None),
        P(None, None, "tensor"),
        P("tensor"),
        P("tensor"),
        P("tensor", None),
        P(),
        P(None, "tensor"),
        P("tensor"),
        P("tensor", None),
        P(),
        P(),
        P(),
        P(),
        P(),
        P(),
    )
    return jax.shard_map(
        per_device, mesh=mesh, in_specs=in_specs, out_specs=out_specs, check_vma=False
    )
```

```python
import functools
import math

import jax
import jax.numpy as jnp
from jax import lax
from jax.experimental import pallas as pl
from jax.experimental.pallas import tpu as pltpu
from jax.sharding import PartitionSpec as P


HEAD_DIM = 64
PASSES = 5
LEN = 192
EPSILON = 1e-05
MASKED = -1e30
QUERY_TILE = 256
LANES = 128
F32 = jnp.float32
BF16 = jnp.bfloat16


def tiles_of(slots):
    return [(q0, min(q0 + QUERY_TILE, slots)) for q0 in range(0, slots, QUERY_TILE)]


def rows_in(slots):
    return [(r0, min(r0 + 240, slots)) for r0 in range(0, slots, 240)]


def dot_nt(a, b):
    return lax.dot_general(a, b, (((1,), (1,)), ((), ())), preferred_element_type=F32)


def dot_nn(a, b):
    return lax.dot_general(a, b, (((1,), (0,)), ((), ())), preferred_element_type=F32)


def dot_tn(a, b):
    return lax.dot_general(a, b, (((0,), (0,)), ((), ())), preferred_element_type=F32)


def half_lanes(values, half):
    lane = lax.broadcasted_iota(jnp.int32, (1, LANES), 1)
    return jnp.where((lane // HEAD_DIM) == half, values, jnp.zeros_like(values))


def diagonal_mask(q0, rows, live):
    key = lax.broadcasted_iota(jnp.int32, (rows, rows), 0)
    query = lax.broadcasted_iota(jnp.int32, (rows, rows), 1)
    return (key <= query) & (key + q0 < live)


def place_rows(block_ref, part, each, place):
    spread, groups = block_ref.shape[:2]
    for group in range(groups):
        for member in range(spread):
            rows = block_ref[member, group, part * each : (part + 1) * each, :]
            place((group * spread + member) * each, rows)


def attend_kernel(
    each, live_ref, n1_ref, w_ref, bias_ref, q_ref, k_ref, v_ref, o_ref, lse_ref, matrix_ref, vt_ref
):
    slots = n1_ref.shape[0]
    live = live_ref[0]
    pair = pl.program_id(0)

    @pl.when(pair == 0)
    def _():
        for part in range(3):

            def place(first, rows, part=part):
                done = 0
                while done < rows.shape[0]:
                    at = (first + done) % LANES
                    size = min(rows.shape[0] - done, LANES - at)
                    start = part * LANES + at
                    matrix_ref[(first + done) // LANES, start : start + size, :] = rows[done : done + size, :]
                    done += size

            place_rows(w_ref, part, each, place)

    projected = dot_nt(n1_ref[...], matrix_ref[pair])
    q_ref[...] = (projected[:, :LANES] + bias_ref[0, 0:1, :]).astype(BF16)
    k_ref[...] = projected[:, LANES : 2 * LANES].astype(BF16)
    values = projected[:, 2 * LANES :] + bias_ref[0, 1:2, :]
    v_ref[...] = values.astype(BF16)
    vt_ref[...] = values.T.astype(BF16)
    for q0, q1 in tiles_of(slots):
        rows = q1 - q0

        @pl.when(q0 >= live)
        def _():
            o_ref[q0:q1, :] = jnp.zeros((rows, LANES), BF16)
            lse_ref[0, :, q0:q1] = jnp.zeros((2, rows), F32)

        @pl.when(q0 < live)
        def _():
            query = q_ref[q0:q1, :] * jnp.asarray(1.0 / math.sqrt(HEAD_DIM), BF16)
            allowed = diagonal_mask(q0, rows, live)
            outs = []
            for half in range(2):
                one = half_lanes(query, half)
                last = dot_nt(k_ref[q0:q1, :], one)
                last = jnp.where(allowed, last, MASKED)
                peak = jnp.max(last, axis=0, keepdims=True)
                if q0:
                    early = dot_nt(k_ref[0:q0, :], one)
                    peak = jnp.maximum(peak, jnp.max(early, axis=0, keepdims=True))
                last = jnp.exp(last - peak)
                total = jnp.sum(last, axis=0, keepdims=True)
                lanes = slice(half * HEAD_DIM, (half + 1) * HEAD_DIM)
                if q0:
                    early = jnp.exp(early - peak)
                    total = total + jnp.sum(early, axis=0, keepdims=True)
                inverse = 1.0 / total
                out = dot_nn(vt_ref[lanes, q0:q1], (last * inverse).astype(BF16))
                if q0:
                    out = out + dot_nn(vt_ref[lanes, 0:q0], (early * inverse).astype(BF16))
                outs.append(out)
                lse_ref[0, half : half + 1, q0:q1] = peak + jnp.log(total)
            o_ref[q0:q1, :] = jnp.concatenate(outs, axis=0).T.astype(BF16)


def attend_back_kernel(
    each, live_ref, q_ref, k_ref, v_ref, o_ref, lse_ref, matrix_ref, mixed_ref, n1_ref, hid_ref, pass_ref,
    d_ref, xhat_ref, inv_ref, cot_ref, vec_ref, wo_ref,
    gblock_ref, gh_ref, sums_ref, gbias_ref,
    kt_ref, dk_sum, dv_sum, ga_s, gmix_s, gn1_s, dw_s, gproj_s,
):
    slots = q_ref.shape[0]
    width = n1_ref.shape[1]
    pairs = gmix_s.shape[0]
    spread, groups = gblock_ref.shape[:2]
    live = live_ref[0]
    pair = pl.program_id(0)
    scale = 1.0 / math.sqrt(HEAD_DIM)

    def add_rows(place, value):
        sums_ref[place : place + 1, :] += jnp.sum(value, axis=0, keepdims=True)

    @pl.when(pair == 0)
    def _():
        sums_ref[...] = jnp.zeros_like(sums_ref)
        for r0, r1 in rows_in(slots):
            grad_n2 = d_ref[r0:r1, :]
            xhat = xhat_ref[r0:r1, :]
            alive = lax.broadcasted_iota(jnp.int32, (r1 - r0, 1), 0) + r0 < live
            grad_y = jnp.where(alive, cot_ref[r0:r1, :].astype(F32), 0.0)
            grad_a = grad_y + norm_back(grad_n2, xhat, inv_ref[r0:r1, :], vec_ref[1:2, :])
            ga_s[r0:r1, :] = grad_a
            grad_att = grad_a.astype(BF16)
            gh_ref[r0:r1, :] = grad_att
            grad_mixed = dot_nt(grad_att, wo_ref[...]).astype(BF16)
            for number in range(pairs):
                gmix_s[number, r0:r1, :] = grad_mixed[:, number * LANES : (number + 1) * LANES]
            for place, value in enumerate((grad_n2 * xhat, grad_n2, grad_a, grad_y)):
                add_rows(2 + place, value)
        grad_out = dot_tn(mixed_ref[...], gh_ref[...]).astype(BF16)
        for group in range(groups):
            for member in range(spread):
                first = (group * spread + member) * each
                gblock_ref[member, group, 3 * each : 4 * each, :] = grad_out[first : first + each, :]
                gblock_ref[member, group, 4 * each :, :] = jnp.zeros(
                    (gblock_ref.shape[2] - 4 * each, width), BF16
                )
        gn1_s[...] = jnp.zeros_like(gn1_s)

    kt_ref[...] = k_ref[...].T
    dk_sum[...] = jnp.zeros_like(dk_sum)
    dv_sum[...] = jnp.zeros_like(dv_sum)
    for q0, q1 in tiles_of(slots):
        rows = q1 - q0

        @pl.when(q0 >= live)
        def _():
            gproj_s[q0:q1, :LANES] = jnp.zeros((rows, LANES), BF16)

        @pl.when(q0 < live)
        def _():
            query = q_ref[q0:q1, :] * jnp.asarray(scale, BF16)
            grad = gmix_s[pair, q0:q1, :]
            allowed = diagonal_mask(q0, rows, live)
            both = (grad.astype(F32) * o_ref[q0:q1, :].astype(F32)).T
            parts = []
            for half in range(2):
                lanes = slice(half * HEAD_DIM, (half + 1) * HEAD_DIM)
                one = half_lanes(query, half)
                grad_one = half_lanes(grad, half)
                lse = lse_ref[0, half : half + 1, q0:q1]
                inner = jnp.sum(both[lanes, :], axis=0, keepdims=True)
                turned = None
                for start, stop in ([(0, q0)] if q0 else []) + [(q0, q1)]:
                    scores = dot_nt(k_ref[start:stop, :], one)
                    probs = jnp.exp(scores - lse)
                    if start == q0:
                        probs = jnp.where(allowed, probs, 0.0)
                    grad_weights = dot_nt(v_ref[start:stop, :], grad_one)
                    grad_scores = (probs * (grad_weights - inner)).astype(BF16)
                    dk_sum[start:stop, :] += dot_nn(grad_scores, one)
                    dv_sum[start:stop, :] += dot_nn(probs.astype(BF16), grad_one)
                    piece = dot_nn(kt_ref[lanes, start:stop], grad_scores)
                    turned = piece if turned is None else turned + piece
                parts.append(turned)
            gproj_s[q0:q1, :LANES] = (jnp.concatenate(parts, axis=0).T * scale).astype(BF16)

    gproj_s[:, LANES : 2 * LANES] = dk_sum[...].astype(BF16)
    gproj_s[:, 2 * LANES :] = dv_sum[...].astype(BF16)
    grad_proj = gproj_s[...]
    dw_s[pair] = dot_tn(grad_proj, n1_ref[...]).astype(BF16)
    gn1_s[...] += dot_nn(grad_proj, matrix_ref[0])
    gbias_ref[0] = jnp.sum(grad_proj.astype(F32), axis=0, keepdims=True)

    @pl.when(pair == pairs - 1)
    def _():
        for r0, r1 in rows_in(slots):
            xhat, inverse = norm_parts(hid_ref[r0:r1, :])
            grad_n1 = gn1_s[r0:r1, :]
            grad_h = ga_s[r0:r1, :] + norm_back(grad_n1, xhat, inverse, vec_ref[4:5, :])
            gh_ref[r0:r1, :] = grad_h.astype(BF16)
            add_rows(0, grad_n1 * xhat)
            add_rows(1, grad_n1)
            passes = pass_ref[r0:r1, :]
            for number in range(PASSES):
                add_rows(6 + number, jnp.where(passes == number, grad_h, 0.0))
        for part in range(3):
            for group in range(groups):
                for member in range(spread):
                    first = (group * spread + member) * each
                    done = 0
                    while done < each:
                        at = (first + done) % LANES
                        size = min(each - done, LANES - at)
                        start = part * LANES + at
                        gblock_ref[member, group, part * each + done : part * each + done + size, :] = dw_s[
                            (first + done) // LANES, start : start + size, :
                        ]
                        done += size


def pair_spec(slots):
    return pl.BlockSpec((slots, LANES), lambda p, live: (0, p))


def attend(live, n1, blocks, biases, each):
    slots, width = n1.shape
    pairs = width // LANES
    spec = pair_spec(slots)
    lse_spec = pl.BlockSpec((1, 2, slots), lambda p, live: (p, 0, 0))
    flops = 2 * 2 * slots * slots * width + 2 * slots * width * 3 * width
    shape = jax.ShapeDtypeStruct((slots, width), BF16)
    return pl.pallas_call(
        functools.partial(attend_kernel, each),
        out_shape=(
            shape,
            shape,
            shape,
            shape,
            jax.ShapeDtypeStruct((pairs, 2, slots), F32),
            jax.ShapeDtypeStruct((pairs, 3 * LANES, width), BF16),
        ),
        grid_spec=pltpu.PrefetchScalarGridSpec(
            num_scalar_prefetch=1,
            grid=(pairs,),
            in_specs=[
                pl.BlockSpec((slots, width), lambda p, live: (0, 0), pipeline_mode=pl.Buffered(1)),
                pl.BlockSpec(blocks.shape, lambda p, live: (0, 0, 0, 0), pipeline_mode=pl.Buffered(1)),
                pl.BlockSpec((1, 2, LANES), lambda p, live: (p, 0, 0)),
            ],
            out_specs=(
                spec,
                spec,
                spec,
                spec,
                lse_spec,
                pl.BlockSpec((pairs, 3 * LANES, width), lambda p, live: (0, 0, 0), pipeline_mode=pl.Buffered(1)),
            ),
            scratch_shapes=[pltpu.VMEM((LANES, slots), BF16)],
        ),
        cost_estimate=pl.CostEstimate(
            flops=flops, transcendentals=slots * slots * width // HEAD_DIM, bytes_accessed=16 * slots * width
        ),
        name="attend",
    )(live, n1, blocks, biases)


def attend_back(
    live, query, keys, values, mixed, lse, matrix, n1, hidden, passes, grad_n2, xhat, inverse, cot, vectors, w_out,
    spread, groups, extra,
):
    slots, width = query.shape
    pairs = width // LANES
    each = width // (spread * groups)
    one = pl.Buffered(1)
    spec = pair_spec(slots)

    def whole(shape):
        return pl.BlockSpec(shape, lambda p, live: (0,) * len(shape), pipeline_mode=one)

    full = whole((slots, width))
    column = whole((slots, 1))
    flops = 5 * 2 * slots * slots * width + 2 * slots * width * 8 * width
    return pl.pallas_call(
        functools.partial(attend_back_kernel, each),
        out_shape=(
            jax.ShapeDtypeStruct((spread, groups, 4 * each + extra, width), BF16),
            jax.ShapeDtypeStruct((slots, width), BF16),
            jax.ShapeDtypeStruct((16, width), F32),
            jax.ShapeDtypeStruct((pairs, 1, 3 * LANES), F32),
        ),
        grid_spec=pltpu.PrefetchScalarGridSpec(
            num_scalar_prefetch=1,
            grid=(pairs,),
            in_specs=[
                spec,
                spec,
                spec,
                spec,
                pl.BlockSpec((1, 2, slots), lambda p, live: (p, 0, 0)),
                pl.BlockSpec((1, 3 * LANES, width), lambda p, live: (p, 0, 0)),
                full,
                full,
                full,
                column,
                full,
                full,
                column,
                full,
                whole((8, width)),
                whole((width, width)),
            ],
            out_specs=(
                whole((spread, groups, 4 * each + extra, width)),
                full,
                whole((16, width)),
                pl.BlockSpec((1, 1, 3 * LANES), lambda p, live: (p, 0, 0)),
            ),
            scratch_shapes=[
                pltpu.VMEM((LANES, slots), BF16),
                pltpu.VMEM((slots, LANES), F32),
                pltpu.VMEM((slots, LANES), F32),
                pltpu.VMEM((slots, width), F32),
                pltpu.VMEM((pairs, slots, LANES), BF16),
                pltpu.VMEM((slots, width), F32),
                pltpu.VMEM((pairs, 3 * LANES, width), BF16),
                pltpu.VMEM((slots, 3 * LANES), BF16),
            ],
        ),
        cost_estimate=pl.CostEstimate(
            flops=flops, transcendentals=slots * slots * width // HEAD_DIM, bytes_accessed=40 * slots * width
        ),
        name="attend_back",
    )(
        live, query, keys, values, mixed, lse, matrix, mixed, n1, hidden, passes, grad_n2, xhat, inverse, cot,
        vectors, w_out,
    )


def ring_pairs(size, shift):
    return [(source, (source + shift) % size) for source in range(size)]


def to_sequence(block, hold=None):
    size = lax.axis_size("tensor")
    me = lax.axis_index("tensor")
    rows, _, width = block.shape
    block = lax.optimization_barrier(block.transpose(1, 0, 2))
    pieces = []
    for shift in range(size):
        piece = lax.dynamic_index_in_dim(block, (me + shift) % size, 0, keepdims=False)
        pieces.append(lax.ppermute(piece, "tensor", ring_pairs(size, shift)) if shift else piece)
    if hold is not None:
        pieces, hold = lax.optimization_barrier((pieces, hold))
    out = jnp.zeros((size * rows, width), block.dtype)
    for shift, piece in enumerate(pieces):
        out = lax.dynamic_update_slice(out, piece, (((me - shift) % size) * rows, 0))
    return (out, hold) if hold is not None else out


def to_slots(values):
    size = lax.axis_size("tensor")
    me = lax.axis_index("tensor")
    slots, width = values.shape
    rows = slots // size
    out = jnp.zeros((slots, width), values.dtype)
    for shift in range(size):
        piece = lax.dynamic_slice(values, (((me + shift) % size) * rows, 0), (rows, width))
        if shift:
            piece = lax.ppermute(piece, "tensor", ring_pairs(size, shift))
        out = lax.dynamic_update_slice(out, piece, (((me - shift) % size) * rows, 0))
    return lax.optimization_barrier(out).reshape(size, rows, width).transpose(1, 0, 2)


def gather_tensor(piece):
    size = lax.axis_size("tensor")
    me = lax.axis_index("tensor")
    rows, width = piece.shape
    out = jnp.zeros((size * rows, width), piece.dtype)
    for shift in range(size):
        other = lax.ppermute(piece, "tensor", ring_pairs(size, shift)) if shift else piece
        out = lax.dynamic_update_slice(out, other, (((me - shift) % size) * rows, 0))
    return out.reshape(size, rows, width)


def gather_batch(piece):
    size = lax.axis_size("batch")
    if size != 8:
        return lax.all_gather(piece, "batch", axis=0, tiled=False)
    me = lax.axis_index("batch")
    rows, width = piece.shape
    out = jnp.zeros((size * rows, width), piece.dtype)
    for turn in range(size):
        other = lax.ppermute(piece, "batch", [(place, place ^ turn) for place in range(size)]) if turn else piece
        out = lax.dynamic_update_slice(out, other, ((me ^ turn) * rows, 0))
    return out.reshape(size, rows, width)


def share(rows):
    size = lax.axis_size("batch")
    each = rows.shape[0] // size
    return lax.dynamic_slice(rows, (lax.axis_index("batch") * each, 0), (each, rows.shape[1]))


def norm_parts(values):
    mean = jnp.mean(values, axis=-1, keepdims=True)
    center = values - mean
    spread = jnp.mean(center * center, axis=-1, keepdims=True)
    inverse = lax.rsqrt(spread + EPSILON)
    return center * inverse, inverse


def norm_back(grad, xhat, inverse, gain):
    scaled = grad * gain
    first = jnp.mean(scaled, axis=-1, keepdims=True)
    second = jnp.mean(scaled * xhat, axis=-1, keepdims=True)
    return inverse * (scaled - first - xhat * second)


def gelu_parts(values):
    outer = math.sqrt(2.0 / math.pi)
    inside = jnp.tanh(outer * (values + 0.044715 * values * values * values))
    act = 0.5 * values * (1.0 + inside)
    slope = 0.5 * (1.0 + inside) + 0.5 * values * (1.0 - inside * inside) * outer * (
        1.0 + 3.0 * 0.044715 * values * values
    )
    return act, slope


def mlp_kernel(
    live_ref, hid_ref, mix_ref, out_ref, cot_ref, vec_ref, bup_ref, up_ref, down_ref,
    y_ref, d_s, xhat_s, inv_s, wo_s, gblock_ref, gbup_ref,
    n2_s, y_s, gm_s,
):
    slots = hid_ref.shape[0]
    step = pl.program_id(0)
    live = live_ref[0]

    def live_rows(r0, r1):
        return lax.broadcasted_iota(jnp.int32, (r1 - r0, 1), 0) + r0 < live

    @pl.when(step == 0)
    def _():
        def place(first, rows):
            wo_s[first : first + rows.shape[0], :] = rows

        place_rows(out_ref, 0, out_ref.shape[2], place)
        for r0, r1 in rows_in(slots):
            after = hid_ref[r0:r1, :] + dot_nn(mix_ref[r0:r1, :], wo_s[...]) + vec_ref[0:1, :]
            xhat, inverse = norm_parts(after)
            xhat_s[r0:r1, :] = xhat
            inv_s[r0:r1, :] = inverse
            n2_s[r0:r1, :] = (xhat * vec_ref[1:2, :] + vec_ref[2:3, :]).astype(BF16)
            y_s[r0:r1, :] = after + vec_ref[3:4, :]
            cot = cot_ref[r0:r1, :]
            gm_s[r0:r1, :] = jnp.where(live_rows(r0, r1), cot, jnp.zeros_like(cot))
            d_s[r0:r1, :] = jnp.zeros((r1 - r0, d_s.shape[1]), F32)

    _, count, units, width = up_ref.shape
    up = up_ref[...].reshape(count * units, width)
    down = down_ref[...].reshape(count * units, width)
    n2 = n2_s[...]
    grad_m = gm_s[...]
    act, slope = gelu_parts(dot_nt(n2, up) + bup_ref[...])
    act = act.astype(BF16)
    grad_u = (dot_nt(grad_m, down) * slope).astype(BF16)
    y_s[...] += dot_nn(act, down)
    d_s[...] += dot_nn(grad_u, up)
    gblock_ref[0, :, 0:units, :] = dot_tn(grad_u, n2).reshape(count, units, width).astype(BF16)
    gblock_ref[0, :, units : 2 * units, :] = dot_tn(act, grad_m).reshape(count, units, width).astype(BF16)
    gbup_ref[...] = jnp.sum(grad_u.astype(F32), axis=0, keepdims=True)

    @pl.when(step == pl.num_programs(0) - 1)
    def _():
        for r0, r1 in rows_in(slots):
            y_ref[r0:r1, :] = jnp.where(live_rows(r0, r1), y_s[r0:r1, :], 0.0).astype(BF16)


def mlp(live, hidden, mixed, cot, vectors, bias_up, blocks, each):
    slots, width = hidden.shape
    steps, groups = blocks.shape[:2]
    units = 4 * each
    chunk = groups * units
    one = pl.Buffered(1)

    def whole(shape):
        return pl.BlockSpec(shape, lambda c, live: (0,) * len(shape), pipeline_mode=one)

    full = whole((slots, width))
    flops = 2 * slots * width * (6 * chunk * steps + 3 * width)
    return pl.pallas_call(
        mlp_kernel,
        out_shape=(
            jax.ShapeDtypeStruct((slots, width), BF16),
            jax.ShapeDtypeStruct((slots, width), F32),
            jax.ShapeDtypeStruct((slots, width), F32),
            jax.ShapeDtypeStruct((slots, 1), F32),
            jax.ShapeDtypeStruct((width, width), BF16),
            jax.ShapeDtypeStruct((steps, groups, 2 * units, width), BF16),
            jax.ShapeDtypeStruct((1, steps * chunk), F32),
        ),
        grid_spec=pltpu.PrefetchScalarGridSpec(
            num_scalar_prefetch=1,
            grid=(steps,),
            in_specs=[
                full,
                full,
                pl.BlockSpec((steps, groups, each, width), lambda c, live: (0, 0, 8, 0), pipeline_mode=one),
                full,
                whole((8, width)),
                pl.BlockSpec((1, chunk), lambda c, live: (0, c)),
                pl.BlockSpec((1, groups, units, width), lambda c, live: (c, 0, 0, 0)),
                pl.BlockSpec((1, groups, units, width), lambda c, live: (c, 0, 1, 0)),
            ],
            out_specs=(
                full,
                full,
                full,
                whole((slots, 1)),
                whole((width, width)),
                pl.BlockSpec((1, groups, 2 * units, width), lambda c, live: (c, 0, 0, 0)),
                pl.BlockSpec((1, chunk), lambda c, live: (0, c)),
            ),
            scratch_shapes=[
                pltpu.VMEM((slots, width), BF16),
                pltpu.VMEM((slots, width), F32),
                pltpu.VMEM((slots, width), BF16),
            ],
        ),
        cost_estimate=pl.CostEstimate(
            flops=flops, transcendentals=slots * steps * chunk, bytes_accessed=20 * slots * width + 8 * steps * chunk * width
        ),
        name="mlp",
    )(live, hidden, mixed, blocks, cot, vectors, bias_up, blocks, blocks)


def layer(
    slot_states,
    pass_counts,
    w_qkv,
    q_bias,
    v_bias,
    w_out,
    out_bias,
    w_up,
    up_bias,
    w_down,
    down_bias,
    ln1_gain,
    ln1_bias,
    ln2_gain,
    ln2_bias,
    pass_table,
    cotangent,
):
    groups = lax.axis_size("tensor")
    spread = lax.axis_size("batch")
    me = lax.axis_index("tensor")
    rows, seqs, width = slot_states.shape
    slots = rows * groups
    hidden_here = w_up.shape[1]
    hidden_units = hidden_here * groups
    assert seqs == groups

    gain_one, shift_one = ln1_gain.astype(F32), ln1_bias.astype(F32)
    gain_two, shift_two = ln2_gain.astype(F32), ln2_bias.astype(F32)
    table = pass_table.astype(F32)

    each = width // (groups * spread)
    units = hidden_here // spread
    here = q_bias.shape[0]
    biases = jnp.concatenate([q_bias, v_bias, jnp.zeros((width - 2 * here,), BF16)]).reshape(1, width)
    qkv_rows = w_qkv.transpose(1, 2, 0)
    qkv_piece = jnp.concatenate(
        [share(qkv_rows[part]) for part in range(3)] + [jnp.pad(biases, ((0, 7), (0, 0)))], axis=0
    )
    qkv_blocks = lax.all_gather(gather_tensor(qkv_piece), "batch", axis=0, tiled=False)
    bias_row = jnp.pad(up_bias.reshape(1, width), ((0, 7), (0, 0)))
    mlp_piece = jnp.concatenate([share(w_up.T), share(w_down), share(w_out), bias_row], axis=0)
    mlp_blocks = lax.all_gather(gather_tensor(mlp_piece), "batch", axis=0, tiled=False)
    states = to_sequence(slot_states).astype(F32)

    bias_rows = qkv_blocks[0, :, 3 * each].astype(F32)
    bias_pairs = jnp.stack(
        [bias_rows[:, part * here : (part + 1) * here].reshape(width // LANES, LANES) for part in range(2)], axis=1
    )
    bias_up = mlp_blocks[0, :, 2 * units + each].reshape(groups, spread, units)

    fold = spread if units % 32 == 0 else 8
    if fold != spread:

        def regrouped(values, first, rows):
            rows_of = values[:, :, first : first + rows].transpose(1, 0, 2, 3)
            return rows_of.reshape(groups, fold, -1, width).transpose(1, 0, 2, 3)

        qkv_blocks = jnp.concatenate([regrouped(qkv_blocks, part * each, each) for part in range(3)], axis=2)
        mlp_blocks = jnp.concatenate(
            [
                regrouped(mlp_blocks, 0, units),
                regrouped(mlp_blocks, units, units),
                regrouped(mlp_blocks, 2 * units, each),
            ],
            axis=2,
        )
        bias_up = bias_up.reshape(groups, fold, -1)
    bias_up = bias_up.transpose(1, 0, 2).reshape(1, hidden_units).astype(F32)

    count = lax.dynamic_index_in_dim(pass_counts, me, 0, keepdims=False)
    index = jnp.arange(slots, dtype=jnp.int32)
    passes = (index % count)[:, None]
    live_count = count * LEN
    live_arg = live_count.reshape(1).astype(jnp.int32)
    added = jnp.zeros((slots, width), F32)
    for number in range(PASSES):
        added = jnp.where(passes == number, table[number][None, :], added)
    hidden = states + added

    xhat_one, _ = norm_parts(hidden)
    n1 = (xhat_one * gain_one + shift_one).astype(BF16)
    n1, hidden, passes, cotangent = lax.optimization_barrier((n1, hidden, passes, cotangent))
    fold_each = width // (groups * fold)
    query, keys, values, mixed, lse, matrix = attend(live_arg, n1, qkv_blocks, bias_pairs, fold_each)
    cot, mixed = to_sequence(cotangent, mixed)
    vectors = jnp.stack([out_bias.astype(F32), gain_two, shift_two, down_bias.astype(F32), gain_one])
    vectors = jnp.pad(vectors, ((0, 3), (0, 0)))
    layer_out, grad_n2, xhat_two, inverse_two, matrix_out, mlp_block, grad_bias_up = mlp(
        live_arg, hidden, mixed, cot, vectors, bias_up, mlp_blocks, fold_each
    )
    if fold != spread:
        mlp_block = mlp_block.reshape(fold, groups, 2, -1, width).transpose(1, 2, 0, 3, 4)
        mlp_block = mlp_block.reshape(groups, 2, spread, units, width).transpose(2, 0, 1, 3, 4)
        mlp_block = mlp_block.reshape(spread, groups, 2 * units, width)
    layer_part = to_slots(layer_out)
    extra = 16
    attn_block, grad_h, sums, grad_bias = attend_back(
        live_arg, query, keys, values, mixed, lse, matrix, n1, hidden, passes, grad_n2, xhat_two, inverse_two, cot,
        vectors, matrix_out, fold, groups, extra,
    )
    grad_part = to_slots(grad_h)

    grad_bias_up = grad_bias_up.reshape(fold, groups, -1).transpose(1, 0, 2).reshape(groups, 1, hidden_here)
    lead = 6 + PASSES
    own = jnp.concatenate(
        [
            grad_bias[:, 0, :LANES].reshape(groups, 1, here),
            grad_bias[:, 0, 2 * LANES :].reshape(groups, 1, here),
            jnp.zeros((groups, 1, width - 2 * here), F32),
        ],
        axis=2,
    )
    small = jnp.concatenate(
        [jnp.broadcast_to(sums[None, :lead], (groups, lead, width)), own, grad_bias_up], axis=1
    )
    small = jnp.pad(small, ((0, 0), (0, spread * extra - lead - 2), (0, 0)))
    small = small.reshape(groups, spread, extra, width).transpose(1, 0, 2, 3).astype(BF16)
    if fold != spread:
        attn_block = attn_block[:, :, : 4 * fold_each].reshape(fold, groups, 4, fold_each, width)
        attn_block = attn_block.transpose(1, 2, 0, 3, 4).reshape(groups, 4, spread, each, width)
        attn_block = attn_block.transpose(2, 0, 1, 3, 4).reshape(spread, groups, 4 * each, width)
        attn_block = jnp.pad(attn_block, ((0, 0), (0, 0), (0, extra), (0, 0)))
    attn_block = lax.dynamic_update_slice(attn_block, small, (0, 0, 4 * each, 0))

    def over_tensor(value):
        kept = lax.dynamic_index_in_dim(value, me, 0, keepdims=False).astype(F32)
        for shift in range(1, groups):
            piece = lax.dynamic_index_in_dim(value, (me + shift) % groups, 0, keepdims=False)
            kept = kept + lax.ppermute(piece, "tensor", ring_pairs(groups, shift)).astype(F32)
        return kept.astype(BF16)

    mlp_block = lax.psum_scatter(mlp_block, "batch", scatter_dimension=0, tiled=True)[0]
    attn_block, mlp_block = lax.optimization_barrier((attn_block, mlp_block))
    attn_block = lax.psum_scatter(attn_block, "batch", scatter_dimension=0, tiled=True)[0]
    mlp_piece = over_tensor(mlp_block)
    attn_piece = over_tensor(attn_block)
    mlp_whole = lax.all_gather(mlp_piece, "batch", axis=0, tiled=False)
    attn_whole = gather_batch(attn_piece)
    parts = [attn_whole[:, part * each : (part + 1) * each].reshape(here, width).astype(F32) for part in range(4)]
    small = attn_whole[:, 4 * each :].reshape(spread * extra, width).astype(F32)
    out_up = mlp_whole[:, :units].reshape(hidden_here, width).astype(F32).T
    out_down = mlp_whole[:, units:].reshape(hidden_here, width).astype(F32)
    out_qkv = jnp.stack(parts[:3], axis=0).transpose(2, 0, 1)
    return (
        layer_part,
        grad_part,
        out_qkv,
        small[lead, :here],
        small[lead, here : 2 * here],
        parts[3],
        small[4],
        out_up,
        small[lead + 1],
        out_down,
        small[5],
        small[0],
        small[1],
        small[2],
        small[3],
        small[6:lead],
    )


def solution(mesh):
    in_specs = (
        P("tensor", "batch", None),
        P("batch"),
        P(None, None, "tensor"),
        P("tensor"),
        P("tensor"),
        P("tensor", None),
        P(),
        P(None, "tensor"),
        P("tensor"),
        P("tensor", None),
        P(),
        P(),
        P(),
        P(),
        P(),
        P(),
        P("tensor", "batch", None),
    )
    out_specs = (
        P("tensor", "batch", None),
        P("tensor", "batch", None),
        P(None, None, "tensor"),
        P("tensor"),
        P("tensor"),
        P("tensor", None),
        P(),
        P(None, "tensor"),
        P("tensor"),
        P("tensor", None),
        P(),
        P(),
        P(),
        P(),
        P(),
        P(),
    )
    return jax.shard_map(layer, mesh=mesh, in_specs=in_specs, out_specs=out_specs, check_vma=False)
```

```python
import functools
import math

import jax
import jax.numpy as jnp
from jax import lax
from jax.experimental import pallas as pl
from jax.experimental.pallas import tpu as pltpu
from jax.sharding import PartitionSpec as P


HEAD_DIM = 64
PASSES = 5
LEN = 192
EPSILON = 1e-05
MASKED = -1e30
QUERY_TILE = 480
TAKE = 2
LANES = 128
F32 = jnp.float32
BF16 = jnp.bfloat16


def tiles_of(slots):
    return [(q0, min(q0 + QUERY_TILE, slots)) for q0 in range(0, slots, QUERY_TILE)]


def rows_in(slots):
    return [(r0, min(r0 + 240, slots)) for r0 in range(0, slots, 240)]


def dot_nt(a, b):
    return lax.dot_general(a, b, (((1,), (1,)), ((), ())), preferred_element_type=F32)


def dot_nn(a, b):
    return lax.dot_general(a, b, (((1,), (0,)), ((), ())), preferred_element_type=F32)


def dot_tn(a, b):
    return lax.dot_general(a, b, (((0,), (0,)), ((), ())), preferred_element_type=F32)


def half_lanes(values, half):
    lane = lax.broadcasted_iota(jnp.int32, (1, LANES), 1)
    return jnp.where((lane // HEAD_DIM) == half, values, jnp.zeros_like(values))


def diagonal_mask(q0, rows, live):
    key = lax.broadcasted_iota(jnp.int32, (rows, rows), 0)
    query = lax.broadcasted_iota(jnp.int32, (rows, rows), 1)
    return (key <= query) & (key + q0 < live)


def place_rows(block_ref, part, each, place):
    spread, groups = block_ref.shape[:2]
    for group in range(groups):
        for member in range(spread):
            rows = block_ref[member, group, part * each : (part + 1) * each, :]
            place((group * spread + member) * each, rows)


def attend_kernel(
    each, live_ref, n1_ref, w_ref, bias_ref, q_ref, k_ref, v_ref, o_ref, lse_ref, matrix_ref, vt_ref
):
    slots = n1_ref.shape[0]
    live = live_ref[0]
    pair = pl.program_id(0)

    @pl.when(pair == 0)
    def _():
        for part in range(3):

            def place(first, rows, part=part):
                done = 0
                while done < rows.shape[0]:
                    at = (first + done) % LANES
                    size = min(rows.shape[0] - done, LANES - at)
                    start = part * LANES + at
                    matrix_ref[(first + done) // LANES, start : start + size, :] = rows[done : done + size, :]
                    done += size

            place_rows(w_ref, part, each, place)

    projected = dot_nt(n1_ref[...], matrix_ref[pair])
    q_ref[...] = (projected[:, :LANES] + bias_ref[0, 0:1, :]).astype(BF16)
    k_ref[...] = projected[:, LANES : 2 * LANES].astype(BF16)
    values = projected[:, 2 * LANES :] + bias_ref[0, 1:2, :]
    v_ref[...] = values.astype(BF16)
    vt_ref[...] = values.T.astype(BF16)
    for q0, q1 in tiles_of(slots):
        rows = q1 - q0

        @pl.when(q0 >= live)
        def _():
            o_ref[q0:q1, :] = jnp.zeros((rows, LANES), BF16)
            lse_ref[0, :, q0:q1] = jnp.zeros((2, rows), F32)

        @pl.when(q0 < live)
        def _():
            query = q_ref[q0:q1, :] * jnp.asarray(1.0 / math.sqrt(HEAD_DIM), BF16)
            allowed = diagonal_mask(q0, rows, live)
            outs = []
            for half in range(2):
                one = half_lanes(query, half)
                last = dot_nt(k_ref[q0:q1, :], one)
                last = jnp.where(allowed, last, MASKED)
                peak = jnp.max(last, axis=0, keepdims=True)
                if q0:
                    early = dot_nt(k_ref[0:q0, :], one)
                    peak = jnp.maximum(peak, jnp.max(early, axis=0, keepdims=True))
                last = jnp.exp(last - peak)
                total = jnp.sum(last, axis=0, keepdims=True)
                lanes = slice(half * HEAD_DIM, (half + 1) * HEAD_DIM)
                if q0:
                    early = jnp.exp(early - peak)
                    total = total + jnp.sum(early, axis=0, keepdims=True)
                out = dot_nn(vt_ref[lanes, q0:q1], last.astype(BF16))
                if q0:
                    out = out + dot_nn(vt_ref[lanes, 0:q0], early.astype(BF16))
                outs.append(out / total)
                lse_ref[0, half : half + 1, q0:q1] = peak + jnp.log(total)
            o_ref[q0:q1, :] = jnp.concatenate(outs, axis=0).T.astype(BF16)


def attend_back_kernel(
    each, live_ref, q_ref, k_ref, v_ref, o_ref, lse_ref, matrix_ref, mixed_ref, n1_ref, hid_ref, pass_ref,
    d_ref, xhat_ref, inv_ref, cot_ref, vec_ref, wo_ref,
    gblock_ref, gh_ref, sums_ref, gbias_ref,
    kt_ref, dk_sum, dv_sum, ga_s, gmix_s, gn1_s, dw_s, gproj_s,
):
    slots = q_ref.shape[0]
    width = n1_ref.shape[1]
    pairs = gmix_s.shape[0]
    spread, groups = gblock_ref.shape[:2]
    live = live_ref[0]
    pair = pl.program_id(0)
    scale = 1.0 / math.sqrt(HEAD_DIM)

    def add_rows(place, value):
        sums_ref[place : place + 1, :] += jnp.sum(value, axis=0, keepdims=True)

    @pl.when(pair == 0)
    def _():
        sums_ref[...] = jnp.zeros_like(sums_ref)
        for r0, r1 in rows_in(slots):
            grad_n2 = d_ref[r0:r1, :]
            xhat = xhat_ref[r0:r1, :]
            alive = lax.broadcasted_iota(jnp.int32, (r1 - r0, 1), 0) + r0 < live
            grad_y = jnp.where(alive, cot_ref[r0:r1, :].astype(F32), 0.0)
            grad_a = grad_y + norm_back(grad_n2, xhat, inv_ref[r0:r1, :], vec_ref[1:2, :])
            ga_s[r0:r1, :] = grad_a
            grad_att = grad_a.astype(BF16)
            gh_ref[r0:r1, :] = grad_att
            grad_mixed = dot_nt(grad_att, wo_ref[...]).astype(BF16)
            for number in range(pairs):
                gmix_s[number, r0:r1, :] = grad_mixed[:, number * LANES : (number + 1) * LANES]
            for place, value in enumerate((grad_n2 * xhat, grad_n2, grad_a, grad_y)):
                add_rows(2 + place, value)
        grad_out = dot_tn(mixed_ref[...], gh_ref[...]).astype(BF16)
        for group in range(groups):
            for member in range(spread):
                first = (group * spread + member) * each
                gblock_ref[member, group, 3 * each : 4 * each, :] = grad_out[first : first + each, :]
                gblock_ref[member, group, 4 * each :, :] = jnp.zeros(
                    (gblock_ref.shape[2] - 4 * each, width), BF16
                )
        gn1_s[...] = jnp.zeros_like(gn1_s)

    kt_ref[...] = k_ref[...].T
    dk_sum[...] = jnp.zeros_like(dk_sum)
    dv_sum[...] = jnp.zeros_like(dv_sum)
    for q0, q1 in tiles_of(slots):
        rows = q1 - q0

        @pl.when(q0 >= live)
        def _():
            gproj_s[q0:q1, :LANES] = jnp.zeros((rows, LANES), BF16)

        @pl.when(q0 < live)
        def _():
            query = q_ref[q0:q1, :] * jnp.asarray(scale, BF16)
            grad = gmix_s[pair, q0:q1, :]
            allowed = diagonal_mask(q0, rows, live)
            both = (grad.astype(F32) * o_ref[q0:q1, :].astype(F32)).T
            parts = []
            for half in range(2):
                lanes = slice(half * HEAD_DIM, (half + 1) * HEAD_DIM)
                one = half_lanes(query, half)
                grad_one = half_lanes(grad, half)
                lse = lse_ref[0, half : half + 1, q0:q1]
                inner = jnp.sum(both[lanes, :], axis=0, keepdims=True)
                turned = None
                for start, stop in ([(0, q0)] if q0 else []) + [(q0, q1)]:
                    scores = dot_nt(k_ref[start:stop, :], one)
                    probs = jnp.exp(scores - lse)
                    if start == q0:
                        probs = jnp.where(allowed, probs, 0.0)
                    grad_weights = dot_nt(v_ref[start:stop, :], grad_one)
                    grad_scores = (probs * (grad_weights - inner)).astype(BF16)
                    dk_sum[start:stop, :] += dot_nn(grad_scores, one)
                    dv_sum[start:stop, :] += dot_nn(probs.astype(BF16), grad_one)
                    piece = dot_nn(kt_ref[lanes, start:stop], grad_scores)
                    turned = piece if turned is None else turned + piece
                parts.append(turned)
            gproj_s[q0:q1, :LANES] = (jnp.concatenate(parts, axis=0).T * scale).astype(BF16)

    gproj_s[:, LANES : 2 * LANES] = dk_sum[...].astype(BF16)
    gproj_s[:, 2 * LANES :] = dv_sum[...].astype(BF16)
    grad_proj = gproj_s[...]
    dw_s[pair] = dot_tn(grad_proj, n1_ref[...]).astype(BF16)
    gn1_s[...] += dot_nn(grad_proj, matrix_ref[0])
    gbias_ref[0] = jnp.sum(grad_proj.astype(F32), axis=0, keepdims=True)

    @pl.when(pair == pairs - 1)
    def _():
        for r0, r1 in rows_in(slots):
            xhat, inverse = norm_parts(hid_ref[r0:r1, :])
            grad_n1 = gn1_s[r0:r1, :]
            grad_h = ga_s[r0:r1, :] + norm_back(grad_n1, xhat, inverse, vec_ref[4:5, :])
            gh_ref[r0:r1, :] = grad_h.astype(BF16)
            add_rows(0, grad_n1 * xhat)
            add_rows(1, grad_n1)
            passes = pass_ref[r0:r1, :]
            for number in range(PASSES):
                add_rows(6 + number, jnp.where(passes == number, grad_h, 0.0))
        for part in range(3):
            for group in range(groups):
                for member in range(spread):
                    first = (group * spread + member) * each
                    done = 0
                    while done < each:
                        at = (first + done) % LANES
                        size = min(each - done, LANES - at)
                        start = part * LANES + at
                        gblock_ref[member, group, part * each + done : part * each + done + size, :] = dw_s[
                            (first + done) // LANES, start : start + size, :
                        ]
                        done += size


def pair_spec(slots):
    return pl.BlockSpec((slots, LANES), lambda p, live: (0, p))


def attend(live, n1, blocks, biases, each):
    slots, width = n1.shape
    pairs = width // LANES
    spec = pair_spec(slots)
    lse_spec = pl.BlockSpec((1, 2, slots), lambda p, live: (p, 0, 0))
    flops = 2 * 2 * slots * slots * width + 2 * slots * width * 3 * width
    shape = jax.ShapeDtypeStruct((slots, width), BF16)
    return pl.pallas_call(
        functools.partial(attend_kernel, each),
        out_shape=(
            shape,
            shape,
            shape,
            shape,
            jax.ShapeDtypeStruct((pairs, 2, slots), F32),
            jax.ShapeDtypeStruct((pairs, 3 * LANES, width), BF16),
        ),
        grid_spec=pltpu.PrefetchScalarGridSpec(
            num_scalar_prefetch=1,
            grid=(pairs,),
            in_specs=[
                pl.BlockSpec((slots, width), lambda p, live: (0, 0), pipeline_mode=pl.Buffered(1)),
                pl.BlockSpec(blocks.shape, lambda p, live: (0, 0, 0, 0), pipeline_mode=pl.Buffered(1)),
                pl.BlockSpec((1, 2, LANES), lambda p, live: (p, 0, 0)),
            ],
            out_specs=(
                spec,
                spec,
                spec,
                spec,
                lse_spec,
                pl.BlockSpec((pairs, 3 * LANES, width), lambda p, live: (0, 0, 0), pipeline_mode=pl.Buffered(1)),
            ),
            scratch_shapes=[pltpu.VMEM((LANES, slots), BF16)],
        ),
        cost_estimate=pl.CostEstimate(
            flops=flops, transcendentals=slots * slots * width // HEAD_DIM, bytes_accessed=16 * slots * width
        ),
        name="attend",
    )(live, n1, blocks, biases)


def attend_back(
    live, query, keys, values, mixed, lse, matrix, n1, hidden, passes, grad_n2, xhat, inverse, cot, vectors, w_out,
    spread, groups, extra,
):
    slots, width = query.shape
    pairs = width // LANES
    each = width // (spread * groups)
    one = pl.Buffered(1)
    spec = pair_spec(slots)

    def whole(shape):
        return pl.BlockSpec(shape, lambda p, live: (0,) * len(shape), pipeline_mode=one)

    full = whole((slots, width))
    column = whole((slots, 1))
    flops = 5 * 2 * slots * slots * width + 2 * slots * width * 8 * width
    return pl.pallas_call(
        functools.partial(attend_back_kernel, each),
        out_shape=(
            jax.ShapeDtypeStruct((spread, groups, 4 * each + extra, width), BF16),
            jax.ShapeDtypeStruct((slots, width), BF16),
            jax.ShapeDtypeStruct((16, width), F32),
            jax.ShapeDtypeStruct((pairs, 1, 3 * LANES), F32),
        ),
        grid_spec=pltpu.PrefetchScalarGridSpec(
            num_scalar_prefetch=1,
            grid=(pairs,),
            in_specs=[
                spec,
                spec,
                spec,
                spec,
                pl.BlockSpec((1, 2, slots), lambda p, live: (p, 0, 0)),
                pl.BlockSpec((1, 3 * LANES, width), lambda p, live: (p, 0, 0)),
                full,
                full,
                full,
                column,
                full,
                full,
                column,
                full,
                whole((8, width)),
                whole((width, width)),
            ],
            out_specs=(
                whole((spread, groups, 4 * each + extra, width)),
                full,
                whole((16, width)),
                pl.BlockSpec((1, 1, 3 * LANES), lambda p, live: (p, 0, 0)),
            ),
            scratch_shapes=[
                pltpu.VMEM((LANES, slots), BF16),
                pltpu.VMEM((slots, LANES), F32),
                pltpu.VMEM((slots, LANES), F32),
                pltpu.VMEM((slots, width), F32),
                pltpu.VMEM((pairs, slots, LANES), BF16),
                pltpu.VMEM((slots, width), F32),
                pltpu.VMEM((pairs, 3 * LANES, width), BF16),
                pltpu.VMEM((slots, 3 * LANES), BF16),
            ],
        ),
        cost_estimate=pl.CostEstimate(
            flops=flops, transcendentals=slots * slots * width // HEAD_DIM, bytes_accessed=40 * slots * width
        ),
        name="attend_back",
    )(
        live, query, keys, values, mixed, lse, matrix, mixed, n1, hidden, passes, grad_n2, xhat, inverse, cot,
        vectors, w_out,
    )


def ring_pairs(size, shift):
    return [(source, (source + shift) % size) for source in range(size)]


def to_sequence(block, hold=None):
    size = lax.axis_size("tensor")
    me = lax.axis_index("tensor")
    rows, _, width = block.shape
    block = lax.optimization_barrier(block.transpose(1, 0, 2))
    pieces = []
    for shift in range(size):
        piece = lax.dynamic_index_in_dim(block, (me + shift) % size, 0, keepdims=False)
        pieces.append(lax.ppermute(piece, "tensor", ring_pairs(size, shift)) if shift else piece)
    if hold is not None:
        pieces, hold = lax.optimization_barrier((pieces, hold))
    out = jnp.zeros((size * rows, width), block.dtype)
    for shift, piece in enumerate(pieces):
        out = lax.dynamic_update_slice(out, piece, (((me - shift) % size) * rows, 0))
    return (out, hold) if hold is not None else out


def to_slots(values):
    size = lax.axis_size("tensor")
    me = lax.axis_index("tensor")
    slots, width = values.shape
    rows = slots // size
    out = jnp.zeros((slots, width), values.dtype)
    for shift in range(size):
        piece = lax.dynamic_slice(values, (((me + shift) % size) * rows, 0), (rows, width))
        if shift:
            piece = lax.ppermute(piece, "tensor", ring_pairs(size, shift))
        out = lax.dynamic_update_slice(out, piece, (((me - shift) % size) * rows, 0))
    return lax.optimization_barrier(out).reshape(size, rows, width).transpose(1, 0, 2)


def gather_tensor(piece):
    size = lax.axis_size("tensor")
    me = lax.axis_index("tensor")
    rows, width = piece.shape
    out = jnp.zeros((size * rows, width), piece.dtype)
    for shift in range(size):
        other = lax.ppermute(piece, "tensor", ring_pairs(size, shift)) if shift else piece
        out = lax.dynamic_update_slice(out, other, (((me - shift) % size) * rows, 0))
    return out.reshape(size, rows, width)


def gather_batch(piece):
    size = lax.axis_size("batch")
    if size != 8:
        return lax.all_gather(piece, "batch", axis=0, tiled=False)
    me = lax.axis_index("batch")
    rows, width = piece.shape
    out = jnp.zeros((size * rows, width), piece.dtype)
    for turn in range(size):
        other = lax.ppermute(piece, "batch", [(place, place ^ turn) for place in range(size)]) if turn else piece
        out = lax.dynamic_update_slice(out, other, ((me ^ turn) * rows, 0))
    return out.reshape(size, rows, width)


def share(rows):
    size = lax.axis_size("batch")
    each = rows.shape[0] // size
    return lax.dynamic_slice(rows, (lax.axis_index("batch") * each, 0), (each, rows.shape[1]))


def norm_parts(values):
    mean = jnp.mean(values, axis=-1, keepdims=True)
    center = values - mean
    spread = jnp.mean(center * center, axis=-1, keepdims=True)
    inverse = lax.rsqrt(spread + EPSILON)
    return center * inverse, inverse


def norm_back(grad, xhat, inverse, gain):
    scaled = grad * gain
    first = jnp.mean(scaled, axis=-1, keepdims=True)
    second = jnp.mean(scaled * xhat, axis=-1, keepdims=True)
    return inverse * (scaled - first - xhat * second)


def gelu_parts(values):
    outer = math.sqrt(2.0 / math.pi)
    inside = jnp.tanh(outer * (values + 0.044715 * values * values * values))
    act = 0.5 * values * (1.0 + inside)
    slope = 0.5 * (1.0 + inside) + 0.5 * values * (1.0 - inside * inside) * outer * (
        1.0 + 3.0 * 0.044715 * values * values
    )
    return act, slope


def mlp_kernel(
    live_ref, hid_ref, mix_ref, out_ref, cot_ref, vec_ref, bup_ref, up_ref, down_ref,
    y_ref, d_s, xhat_s, inv_s, wo_s, gblock_ref, gbup_ref,
    n2_s, y_s, gm_s,
):
    slots = hid_ref.shape[0]
    step = pl.program_id(0)
    live = live_ref[0]

    def live_rows(r0, r1):
        return lax.broadcasted_iota(jnp.int32, (r1 - r0, 1), 0) + r0 < live

    @pl.when(step == 0)
    def _():
        def place(first, rows):
            wo_s[first : first + rows.shape[0], :] = rows

        place_rows(out_ref, 0, out_ref.shape[2], place)
        for r0, r1 in rows_in(slots):
            after = hid_ref[r0:r1, :] + dot_nn(mix_ref[r0:r1, :], wo_s[...]) + vec_ref[0:1, :]
            xhat, inverse = norm_parts(after)
            xhat_s[r0:r1, :] = xhat
            inv_s[r0:r1, :] = inverse
            n2_s[r0:r1, :] = (xhat * vec_ref[1:2, :] + vec_ref[2:3, :]).astype(BF16)
            y_s[r0:r1, :] = after + vec_ref[3:4, :]
            cot = cot_ref[r0:r1, :]
            gm_s[r0:r1, :] = jnp.where(live_rows(r0, r1), cot, jnp.zeros_like(cot))
            d_s[r0:r1, :] = jnp.zeros((r1 - r0, d_s.shape[1]), F32)

    take, count, units, width = up_ref.shape
    up = up_ref[...].reshape(take * count * units, width)
    down = down_ref[...].reshape(take * count * units, width)
    n2 = n2_s[...]
    grad_m = gm_s[...]
    act, slope = gelu_parts(dot_nt(n2, up) + bup_ref[...])
    act = act.astype(BF16)
    grad_u = (dot_nt(grad_m, down) * slope).astype(BF16)
    y_s[...] += dot_nn(act, down)
    d_s[...] += dot_nn(grad_u, up)
    gblock_ref[:, :, 0:units, :] = dot_tn(grad_u, n2).astype(BF16).reshape(take, count, units, width)
    gblock_ref[:, :, units : 2 * units, :] = dot_tn(act, grad_m).astype(BF16).reshape(take, count, units, width)
    gbup_ref[...] = jnp.sum(grad_u.astype(F32), axis=0, keepdims=True)

    @pl.when(step == pl.num_programs(0) - 1)
    def _():
        for r0, r1 in rows_in(slots):
            y_ref[r0:r1, :] = jnp.where(live_rows(r0, r1), y_s[r0:r1, :], 0.0).astype(BF16)


def mlp(live, hidden, mixed, cot, vectors, bias_up, blocks, each):
    slots, width = hidden.shape
    spread, groups = blocks.shape[:2]
    units = 4 * each
    take = TAKE
    steps = spread // take
    chunk = take * groups * units
    one = pl.Buffered(1)

    def whole(shape):
        return pl.BlockSpec(shape, lambda c, live: (0,) * len(shape), pipeline_mode=one)

    full = whole((slots, width))
    flops = 2 * slots * width * (6 * chunk * steps + 3 * width)
    return pl.pallas_call(
        mlp_kernel,
        out_shape=(
            jax.ShapeDtypeStruct((slots, width), BF16),
            jax.ShapeDtypeStruct((slots, width), F32),
            jax.ShapeDtypeStruct((slots, width), F32),
            jax.ShapeDtypeStruct((slots, 1), F32),
            jax.ShapeDtypeStruct((width, width), BF16),
            jax.ShapeDtypeStruct((spread, groups, 2 * units, width), BF16),
            jax.ShapeDtypeStruct((1, steps * chunk), F32),
        ),
        grid_spec=pltpu.PrefetchScalarGridSpec(
            num_scalar_prefetch=1,
            grid=(steps,),
            in_specs=[
                full,
                full,
                pl.BlockSpec((spread, groups, each, width), lambda c, live: (0, 0, 8, 0), pipeline_mode=one),
                full,
                whole((8, width)),
                pl.BlockSpec((1, chunk), lambda c, live: (0, c)),
                pl.BlockSpec((take, groups, units, width), lambda c, live: (c, 0, 0, 0)),
                pl.BlockSpec((take, groups, units, width), lambda c, live: (c, 0, 1, 0)),
            ],
            out_specs=(
                full,
                full,
                full,
                whole((slots, 1)),
                whole((width, width)),
                pl.BlockSpec((take, groups, 2 * units, width), lambda c, live: (c, 0, 0, 0)),
                pl.BlockSpec((1, chunk), lambda c, live: (0, c)),
            ),
            scratch_shapes=[
                pltpu.VMEM((slots, width), BF16),
                pltpu.VMEM((slots, width), F32),
                pltpu.VMEM((slots, width), BF16),
            ],
        ),
        cost_estimate=pl.CostEstimate(
            flops=flops, transcendentals=slots * steps * chunk, bytes_accessed=20 * slots * width + 8 * steps * chunk * width
        ),
        name="mlp",
    )(live, hidden, mixed, blocks, cot, vectors, bias_up, blocks, blocks)


def layer(
    slot_states,
    pass_counts,
    w_qkv,
    q_bias,
    v_bias,
    w_out,
    out_bias,
    w_up,
    up_bias,
    w_down,
    down_bias,
    ln1_gain,
    ln1_bias,
    ln2_gain,
    ln2_bias,
    pass_table,
    cotangent,
):
    groups = lax.axis_size("tensor")
    spread = lax.axis_size("batch")
    me = lax.axis_index("tensor")
    rows, seqs, width = slot_states.shape
    slots = rows * groups
    hidden_here = w_up.shape[1]
    hidden_units = hidden_here * groups
    assert seqs == groups

    gain_one, shift_one = ln1_gain.astype(F32), ln1_bias.astype(F32)
    gain_two, shift_two = ln2_gain.astype(F32), ln2_bias.astype(F32)
    table = pass_table.astype(F32)

    each = width // (groups * spread)
    units = hidden_here // spread
    here = q_bias.shape[0]
    biases = jnp.concatenate([q_bias, v_bias, jnp.zeros((width - 2 * here,), BF16)]).reshape(1, width)
    qkv_rows = w_qkv.transpose(1, 2, 0)
    qkv_piece = jnp.concatenate(
        [share(qkv_rows[part]) for part in range(3)] + [jnp.pad(biases, ((0, 7), (0, 0)))], axis=0
    )
    qkv_blocks = lax.all_gather(gather_tensor(qkv_piece), "batch", axis=0, tiled=False)
    bias_row = jnp.pad(up_bias.reshape(1, width), ((0, 7), (0, 0)))
    mlp_piece = jnp.concatenate([share(w_up.T), share(w_down), share(w_out), bias_row], axis=0)
    mlp_blocks = lax.all_gather(gather_tensor(mlp_piece), "batch", axis=0, tiled=False)
    states = to_sequence(slot_states).astype(F32)

    bias_rows = qkv_blocks[0, :, 3 * each].astype(F32)
    bias_pairs = jnp.stack(
        [bias_rows[:, part * here : (part + 1) * here].reshape(width // LANES, LANES) for part in range(2)], axis=1
    )
    bias_up = mlp_blocks[0, :, 2 * units + each].reshape(groups, spread, units)

    fold = spread if units % 32 == 0 else 8
    if fold != spread:

        def regrouped(values, first, rows):
            rows_of = values[:, :, first : first + rows].transpose(1, 0, 2, 3)
            return rows_of.reshape(groups, fold, -1, width).transpose(1, 0, 2, 3)

        qkv_blocks = jnp.concatenate([regrouped(qkv_blocks, part * each, each) for part in range(3)], axis=2)
        mlp_blocks = jnp.concatenate(
            [
                regrouped(mlp_blocks, 0, units),
                regrouped(mlp_blocks, units, units),
                regrouped(mlp_blocks, 2 * units, each),
            ],
            axis=2,
        )
        bias_up = bias_up.reshape(groups, fold, -1)
    bias_up = bias_up.transpose(1, 0, 2).reshape(1, hidden_units).astype(F32)

    count = lax.dynamic_index_in_dim(pass_counts, me, 0, keepdims=False)
    index = jnp.arange(slots, dtype=jnp.int32)
    passes = (index % count)[:, None]
    live_count = count * LEN
    live_arg = live_count.reshape(1).astype(jnp.int32)
    added = jnp.zeros((slots, width), F32)
    for number in range(PASSES):
        added = jnp.where(passes == number, table[number][None, :], added)
    hidden = states + added

    xhat_one, _ = norm_parts(hidden)
    n1 = (xhat_one * gain_one + shift_one).astype(BF16)
    n1, hidden, passes, cotangent = lax.optimization_barrier((n1, hidden, passes, cotangent))
    fold_each = width // (groups * fold)
    query, keys, values, mixed, lse, matrix = attend(live_arg, n1, qkv_blocks, bias_pairs, fold_each)
    cot, mixed = to_sequence(cotangent, mixed)
    vectors = jnp.stack([out_bias.astype(F32), gain_two, shift_two, down_bias.astype(F32), gain_one])
    vectors = jnp.pad(vectors, ((0, 3), (0, 0)))
    layer_out, grad_n2, xhat_two, inverse_two, matrix_out, mlp_block, grad_bias_up = mlp(
        live_arg, hidden, mixed, cot, vectors, bias_up, mlp_blocks, fold_each
    )
    if fold != spread:
        mlp_block = mlp_block.reshape(fold, groups, 2, -1, width).transpose(1, 2, 0, 3, 4)
        mlp_block = mlp_block.reshape(groups, 2, spread, units, width).transpose(2, 0, 1, 3, 4)
        mlp_block = mlp_block.reshape(spread, groups, 2 * units, width)
    layer_part = to_slots(layer_out)
    extra = 8 if spread * 8 >= 8 + PASSES else 16
    attn_block, grad_h, sums, grad_bias = attend_back(
        live_arg, query, keys, values, mixed, lse, matrix, n1, hidden, passes, grad_n2, xhat_two, inverse_two, cot,
        vectors, matrix_out, fold, groups, extra,
    )
    grad_part = to_slots(grad_h)

    grad_bias_up = grad_bias_up.reshape(fold, groups, -1).transpose(1, 0, 2).reshape(groups, 1, hidden_here)
    lead = 6 + PASSES
    own = jnp.concatenate(
        [
            grad_bias[:, 0, :LANES].reshape(groups, 1, here),
            grad_bias[:, 0, 2 * LANES :].reshape(groups, 1, here),
            jnp.zeros((groups, 1, width - 2 * here), F32),
        ],
        axis=2,
    )
    small = jnp.concatenate(
        [jnp.broadcast_to(sums[None, :lead], (groups, lead, width)), own, grad_bias_up], axis=1
    )
    small = jnp.pad(small, ((0, 0), (0, spread * extra - lead - 2), (0, 0)))
    small = small.reshape(groups, spread, extra, width).transpose(1, 0, 2, 3).astype(BF16)
    if fold != spread:
        attn_block = attn_block[:, :, : 4 * fold_each].reshape(fold, groups, 4, fold_each, width)
        attn_block = attn_block.transpose(1, 2, 0, 3, 4).reshape(groups, 4, spread, each, width)
        attn_block = attn_block.transpose(2, 0, 1, 3, 4).reshape(spread, groups, 4 * each, width)
        attn_block = jnp.pad(attn_block, ((0, 0), (0, 0), (0, extra), (0, 0)))
    attn_block = lax.dynamic_update_slice(attn_block, small, (0, 0, 4 * each, 0))

    def over_tensor(value):
        kept = lax.dynamic_index_in_dim(value, me, 0, keepdims=False).astype(F32)
        for shift in range(1, groups):
            piece = lax.dynamic_index_in_dim(value, (me + shift) % groups, 0, keepdims=False)
            kept = kept + lax.ppermute(piece, "tensor", ring_pairs(groups, shift)).astype(F32)
        return kept.astype(BF16)

    mlp_block = lax.psum_scatter(mlp_block, "batch", scatter_dimension=0, tiled=True)[0]
    attn_block, mlp_block = lax.optimization_barrier((attn_block, mlp_block))
    attn_block = lax.psum_scatter(attn_block, "batch", scatter_dimension=0, tiled=True)[0]
    mlp_piece = over_tensor(mlp_block)
    attn_piece = over_tensor(attn_block)
    mlp_whole = gather_batch(mlp_piece)
    attn_whole = gather_batch(attn_piece)
    parts = [attn_whole[:, part * each : (part + 1) * each].reshape(here, width).astype(F32) for part in range(4)]
    small = attn_whole[:, 4 * each :].reshape(spread * extra, width).astype(F32)
    out_up = mlp_whole[:, :units].reshape(hidden_here, width).astype(F32).T
    out_down = mlp_whole[:, units:].reshape(hidden_here, width).astype(F32)
    out_qkv = jnp.stack(parts[:3], axis=0).transpose(2, 0, 1)
    return (
        layer_part,
        grad_part,
        out_qkv,
        small[lead, :here],
        small[lead, here : 2 * here],
        parts[3],
        small[4],
        out_up,
        small[lead + 1],
        out_down,
        small[5],
        small[0],
        small[1],
        small[2],
        small[3],
        small[6:lead],
    )


def solution(mesh):
    in_specs = (
        P("tensor", "batch", None),
        P("batch"),
        P(None, None, "tensor"),
        P("tensor"),
        P("tensor"),
        P("tensor", None),
        P(),
        P(None, "tensor"),
        P("tensor"),
        P("tensor", None),
        P(),
        P(),
        P(),
        P(),
        P(),
        P(),
        P("tensor", "batch", None),
    )
    out_specs = (
        P("tensor", "batch", None),
        P("tensor", "batch", None),
        P(None, None, "tensor"),
        P("tensor"),
        P("tensor"),
        P("tensor", None),
        P(),
        P(None, "tensor"),
        P("tensor"),
        P("tensor", None),
        P(),
        P(),
        P(),
        P(),
        P(),
        P(),
    )
    return jax.shard_map(layer, mesh=mesh, in_specs=in_specs, out_specs=out_specs, check_vma=False)
```

```python
import functools
import math

import jax
import jax.numpy as jnp
from jax import lax
from jax.experimental import pallas as pl
from jax.experimental.pallas import tpu as pltpu
from jax.sharding import PartitionSpec as P


HEAD_DIM = 64
PASSES = 5
LEN = 192
EPSILON = 1e-05
MASKED = -1e30
QUERY_TILE = 480
TAKE = 2
LANES = 128
F32 = jnp.float32
BF16 = jnp.bfloat16


def tiles_of(slots):
    return [(q0, min(q0 + QUERY_TILE, slots)) for q0 in range(0, slots, QUERY_TILE)]


def rows_in(slots):
    return [(r0, min(r0 + 240, slots)) for r0 in range(0, slots, 240)]


def dot_nt(a, b):
    return lax.dot_general(a, b, (((1,), (1,)), ((), ())), preferred_element_type=F32)


def dot_nn(a, b):
    return lax.dot_general(a, b, (((1,), (0,)), ((), ())), preferred_element_type=F32)


def dot_tn(a, b):
    return lax.dot_general(a, b, (((0,), (0,)), ((), ())), preferred_element_type=F32)


def half_lanes(values, half):
    lane = lax.broadcasted_iota(jnp.int32, (1, LANES), 1)
    return jnp.where((lane // HEAD_DIM) == half, values, jnp.zeros_like(values))


def diagonal_mask(q0, rows, live):
    key = lax.broadcasted_iota(jnp.int32, (rows, rows), 0)
    query = lax.broadcasted_iota(jnp.int32, (rows, rows), 1)
    return (key <= query) & (key + q0 < live)


def place_rows(block_ref, part, each, place):
    spread, groups = block_ref.shape[:2]
    for group in range(groups):
        for member in range(spread):
            rows = block_ref[member, group, part * each : (part + 1) * each, :]
            place((group * spread + member) * each, rows)


def attend_kernel(
    each, live_ref, n1_ref, w_ref, bias_ref, q_ref, k_ref, v_ref, o_ref, lse_ref, matrix_ref, vt_ref
):
    slots = n1_ref.shape[0]
    live = live_ref[0]
    pair = pl.program_id(0)

    @pl.when(pair == 0)
    def _():
        for part in range(3):

            def place(first, rows, part=part):
                done = 0
                while done < rows.shape[0]:
                    at = (first + done) % LANES
                    size = min(rows.shape[0] - done, LANES - at)
                    start = part * LANES + at
                    matrix_ref[(first + done) // LANES, start : start + size, :] = rows[done : done + size, :]
                    done += size

            place_rows(w_ref, part, each, place)

    projected = dot_nt(n1_ref[...], matrix_ref[pair])
    q_ref[...] = (projected[:, :LANES] + bias_ref[0, 0:1, :]).astype(BF16)
    k_ref[...] = projected[:, LANES : 2 * LANES].astype(BF16)
    values = projected[:, 2 * LANES :] + bias_ref[0, 1:2, :]
    v_ref[...] = values.astype(BF16)
    vt_ref[...] = values.T.astype(BF16)
    for q0, q1 in tiles_of(slots):
        rows = q1 - q0

        @pl.when(q0 >= live)
        def _():
            o_ref[q0:q1, :] = jnp.zeros((rows, LANES), BF16)
            lse_ref[0, :, q0:q1] = jnp.zeros((2, rows), F32)

        @pl.when(q0 < live)
        def _():
            query = q_ref[q0:q1, :] * jnp.asarray(1.0 / math.sqrt(HEAD_DIM), BF16)
            allowed = diagonal_mask(q0, rows, live)
            outs = []
            for half in range(2):
                one = half_lanes(query, half)
                last = dot_nt(k_ref[q0:q1, :], one)
                last = jnp.where(allowed, last, MASKED)
                peak = jnp.max(last, axis=0, keepdims=True)
                if q0:
                    early = dot_nt(k_ref[0:q0, :], one)
                    peak = jnp.maximum(peak, jnp.max(early, axis=0, keepdims=True))
                last = jnp.exp(last - peak)
                total = jnp.sum(last, axis=0, keepdims=True)
                lanes = slice(half * HEAD_DIM, (half + 1) * HEAD_DIM)
                if q0:
                    early = jnp.exp(early - peak)
                    total = total + jnp.sum(early, axis=0, keepdims=True)
                out = dot_nn(vt_ref[lanes, q0:q1], last.astype(BF16))
                if q0:
                    out = out + dot_nn(vt_ref[lanes, 0:q0], early.astype(BF16))
                outs.append(out / total)
                lse_ref[0, half : half + 1, q0:q1] = peak + jnp.log(total)
            o_ref[q0:q1, :] = jnp.concatenate(outs, axis=0).T.astype(BF16)


def attend_back_kernel(
    each, live_ref, q_ref, k_ref, v_ref, o_ref, lse_ref, matrix_ref, mixed_ref, n1_ref, hid_ref, pass_ref,
    d_ref, xhat_ref, inv_ref, cot_ref, vec_ref, wo_ref,
    gblock_ref, gh_ref, sums_ref, gbias_ref,
    kt_ref, dk_sum, dv_sum, ga_s, gmix_s, gn1_s, dw_s, gproj_s,
):
    slots = q_ref.shape[0]
    width = n1_ref.shape[1]
    pairs = gmix_s.shape[0]
    spread, groups = gblock_ref.shape[:2]
    live = live_ref[0]
    pair = pl.program_id(0)
    scale = 1.0 / math.sqrt(HEAD_DIM)

    def add_rows(place, value):
        sums_ref[place : place + 1, :] += jnp.sum(value, axis=0, keepdims=True)

    @pl.when(pair == 0)
    def _():
        sums_ref[...] = jnp.zeros_like(sums_ref)
        for r0, r1 in rows_in(slots):
            grad_n2 = d_ref[r0:r1, :]
            xhat = xhat_ref[r0:r1, :]
            alive = lax.broadcasted_iota(jnp.int32, (r1 - r0, 1), 0) + r0 < live
            grad_y = jnp.where(alive, cot_ref[r0:r1, :].astype(F32), 0.0)
            grad_a = grad_y + norm_back(grad_n2, xhat, inv_ref[r0:r1, :], vec_ref[1:2, :])
            ga_s[r0:r1, :] = grad_a
            grad_att = grad_a.astype(BF16)
            gh_ref[r0:r1, :] = grad_att
            grad_mixed = dot_nt(grad_att, wo_ref[...]).astype(BF16)
            for number in range(pairs):
                gmix_s[number, r0:r1, :] = grad_mixed[:, number * LANES : (number + 1) * LANES]
            for place, value in enumerate((grad_n2 * xhat, grad_n2, grad_a, grad_y)):
                add_rows(2 + place, value)
        grad_out = dot_tn(mixed_ref[...], gh_ref[...]).astype(BF16)
        for group in range(groups):
            for member in range(spread):
                first = (group * spread + member) * each
                gblock_ref[member, group, 3 * each : 4 * each, :] = grad_out[first : first + each, :]
                gblock_ref[member, group, 4 * each :, :] = jnp.zeros(
                    (gblock_ref.shape[2] - 4 * each, width), BF16
                )
        gn1_s[...] = jnp.zeros_like(gn1_s)

    kt_ref[...] = k_ref[...].T
    dk_sum[...] = jnp.zeros_like(dk_sum)
    dv_sum[...] = jnp.zeros_like(dv_sum)
    for q0, q1 in tiles_of(slots):
        rows = q1 - q0

        @pl.when(q0 >= live)
        def _():
            gproj_s[q0:q1, :LANES] = jnp.zeros((rows, LANES), BF16)

        @pl.when(q0 < live)
        def _():
            query = q_ref[q0:q1, :] * jnp.asarray(scale, BF16)
            grad = gmix_s[pair, q0:q1, :]
            allowed = diagonal_mask(q0, rows, live)
            both = (grad.astype(F32) * o_ref[q0:q1, :].astype(F32)).T
            parts = []
            for half in range(2):
                lanes = slice(half * HEAD_DIM, (half + 1) * HEAD_DIM)
                one = half_lanes(query, half)
                grad_one = half_lanes(grad, half)
                lse = lse_ref[0, half : half + 1, q0:q1]
                inner = jnp.sum(both[lanes, :], axis=0, keepdims=True)
                turned = None
                for start, stop in ([(0, q0)] if q0 else []) + [(q0, q1)]:
                    scores = dot_nt(k_ref[start:stop, :], one)
                    probs = jnp.exp(scores - lse)
                    if start == q0:
                        probs = jnp.where(allowed, probs, 0.0)
                    grad_weights = dot_nt(v_ref[start:stop, :], grad_one)
                    grad_scores = (probs * (grad_weights - inner)).astype(BF16)
                    dk_sum[start:stop, :] += dot_nn(grad_scores, one)
                    dv_sum[start:stop, :] += dot_nn(probs.astype(BF16), grad_one)
                    piece = dot_nn(kt_ref[lanes, start:stop], grad_scores)
                    turned = piece if turned is None else turned + piece
                parts.append(turned)
            gproj_s[q0:q1, :LANES] = (jnp.concatenate(parts, axis=0).T * scale).astype(BF16)

    gproj_s[:, LANES : 2 * LANES] = dk_sum[...].astype(BF16)
    gproj_s[:, 2 * LANES :] = dv_sum[...].astype(BF16)
    grad_proj = gproj_s[...]
    dw_s[pair] = dot_tn(grad_proj, n1_ref[...]).astype(BF16)
    gn1_s[...] += dot_nn(grad_proj, matrix_ref[0])
    gbias_ref[0] = jnp.sum(grad_proj.astype(F32), axis=0, keepdims=True)

    @pl.when(pair == pairs - 1)
    def _():
        for r0, r1 in rows_in(slots):
            xhat, inverse = norm_parts(hid_ref[r0:r1, :])
            grad_n1 = gn1_s[r0:r1, :]
            grad_h = ga_s[r0:r1, :] + norm_back(grad_n1, xhat, inverse, vec_ref[4:5, :])
            gh_ref[r0:r1, :] = grad_h.astype(BF16)
            add_rows(0, grad_n1 * xhat)
            add_rows(1, grad_n1)
            passes = pass_ref[r0:r1, :]
            for number in range(PASSES):
                add_rows(6 + number, jnp.where(passes == number, grad_h, 0.0))
        for part in range(3):
            for group in range(groups):
                for member in range(spread):
                    first = (group * spread + member) * each
                    done = 0
                    while done < each:
                        at = (first + done) % LANES
                        size = min(each - done, LANES - at)
                        start = part * LANES + at
                        gblock_ref[member, group, part * each + done : part * each + done + size, :] = dw_s[
                            (first + done) // LANES, start : start + size, :
                        ]
                        done += size


def pair_spec(slots):
    return pl.BlockSpec((slots, LANES), lambda p, live: (0, p))


def attend(live, n1, blocks, biases, each):
    slots, width = n1.shape
    pairs = width // LANES
    spec = pair_spec(slots)
    lse_spec = pl.BlockSpec((1, 2, slots), lambda p, live: (p, 0, 0))
    flops = 2 * 2 * slots * slots * width + 2 * slots * width * 3 * width
    shape = jax.ShapeDtypeStruct((slots, width), BF16)
    return pl.pallas_call(
        functools.partial(attend_kernel, each),
        out_shape=(
            shape,
            shape,
            shape,
            shape,
            jax.ShapeDtypeStruct((pairs, 2, slots), F32),
            jax.ShapeDtypeStruct((pairs, 3 * LANES, width), BF16),
        ),
        grid_spec=pltpu.PrefetchScalarGridSpec(
            num_scalar_prefetch=1,
            grid=(pairs,),
            in_specs=[
                pl.BlockSpec((slots, width), lambda p, live: (0, 0), pipeline_mode=pl.Buffered(1)),
                pl.BlockSpec(blocks.shape, lambda p, live: (0, 0, 0, 0), pipeline_mode=pl.Buffered(1)),
                pl.BlockSpec((1, 2, LANES), lambda p, live: (p, 0, 0)),
            ],
            out_specs=(
                spec,
                spec,
                spec,
                spec,
                lse_spec,
                pl.BlockSpec((pairs, 3 * LANES, width), lambda p, live: (0, 0, 0), pipeline_mode=pl.Buffered(1)),
            ),
            scratch_shapes=[pltpu.VMEM((LANES, slots), BF16)],
        ),
        cost_estimate=pl.CostEstimate(
            flops=flops, transcendentals=slots * slots * width // HEAD_DIM, bytes_accessed=16 * slots * width
        ),
        name="attend",
    )(live, n1, blocks, biases)


def attend_back(
    live, query, keys, values, mixed, lse, matrix, n1, hidden, passes, grad_n2, xhat, inverse, cot, vectors, w_out,
    spread, groups, extra,
):
    slots, width = query.shape
    pairs = width // LANES
    each = width // (spread * groups)
    one = pl.Buffered(1)
    spec = pair_spec(slots)

    def whole(shape):
        return pl.BlockSpec(shape, lambda p, live: (0,) * len(shape), pipeline_mode=one)

    full = whole((slots, width))
    column = whole((slots, 1))
    flops = 5 * 2 * slots * slots * width + 2 * slots * width * 8 * width
    return pl.pallas_call(
        functools.partial(attend_back_kernel, each),
        out_shape=(
            jax.ShapeDtypeStruct((spread, groups, 4 * each + extra, width), BF16),
            jax.ShapeDtypeStruct((slots, width), BF16),
            jax.ShapeDtypeStruct((16, width), F32),
            jax.ShapeDtypeStruct((pairs, 1, 3 * LANES), F32),
        ),
        grid_spec=pltpu.PrefetchScalarGridSpec(
            num_scalar_prefetch=1,
            grid=(pairs,),
            in_specs=[
                spec,
                spec,
                spec,
                spec,
                pl.BlockSpec((1, 2, slots), lambda p, live: (p, 0, 0)),
                pl.BlockSpec((1, 3 * LANES, width), lambda p, live: (p, 0, 0)),
                full,
                full,
                full,
                column,
                full,
                full,
                column,
                full,
                whole((8, width)),
                whole((width, width)),
            ],
            out_specs=(
                whole((spread, groups, 4 * each + extra, width)),
                full,
                whole((16, width)),
                pl.BlockSpec((1, 1, 3 * LANES), lambda p, live: (p, 0, 0)),
            ),
            scratch_shapes=[
                pltpu.VMEM((LANES, slots), BF16),
                pltpu.VMEM((slots, LANES), F32),
                pltpu.VMEM((slots, LANES), F32),
                pltpu.VMEM((slots, width), F32),
                pltpu.VMEM((pairs, slots, LANES), BF16),
                pltpu.VMEM((slots, width), F32),
                pltpu.VMEM((pairs, 3 * LANES, width), BF16),
                pltpu.VMEM((slots, 3 * LANES), BF16),
            ],
        ),
        cost_estimate=pl.CostEstimate(
            flops=flops, transcendentals=slots * slots * width // HEAD_DIM, bytes_accessed=40 * slots * width
        ),
        name="attend_back",
    )(
        live, query, keys, values, mixed, lse, matrix, mixed, n1, hidden, passes, grad_n2, xhat, inverse, cot,
        vectors, w_out,
    )


def ring_pairs(size, shift):
    return [(source, (source + shift) % size) for source in range(size)]


def to_sequence(block, hold=None):
    size = lax.axis_size("tensor")
    me = lax.axis_index("tensor")
    rows, _, width = block.shape
    block = lax.optimization_barrier(block.transpose(1, 0, 2))
    pieces = []
    for shift in range(size):
        piece = lax.dynamic_index_in_dim(block, (me + shift) % size, 0, keepdims=False)
        pieces.append(lax.ppermute(piece, "tensor", ring_pairs(size, shift)) if shift else piece)
    if hold is not None:
        pieces, hold = lax.optimization_barrier((pieces, hold))
    out = jnp.zeros((size * rows, width), block.dtype)
    for shift, piece in enumerate(pieces):
        out = lax.dynamic_update_slice(out, piece, (((me - shift) % size) * rows, 0))
    return (out, hold) if hold is not None else out


def to_slots(values):
    size = lax.axis_size("tensor")
    me = lax.axis_index("tensor")
    slots, width = values.shape
    rows = slots // size
    out = jnp.zeros((slots, width), values.dtype)
    for shift in range(size):
        piece = lax.dynamic_slice(values, (((me + shift) % size) * rows, 0), (rows, width))
        if shift:
            piece = lax.ppermute(piece, "tensor", ring_pairs(size, shift))
        out = lax.dynamic_update_slice(out, piece, (((me - shift) % size) * rows, 0))
    return lax.optimization_barrier(out).reshape(size, rows, width).transpose(1, 0, 2)


def gather_tensor(piece):
    size = lax.axis_size("tensor")
    me = lax.axis_index("tensor")
    rows, width = piece.shape
    out = jnp.zeros((size * rows, width), piece.dtype)
    for shift in range(size):
        other = lax.ppermute(piece, "tensor", ring_pairs(size, shift)) if shift else piece
        out = lax.dynamic_update_slice(out, other, (((me - shift) % size) * rows, 0))
    return out.reshape(size, rows, width)


def gather_batch(piece):
    size = lax.axis_size("batch")
    if size != 8:
        return lax.all_gather(piece, "batch", axis=0, tiled=False)
    me = lax.axis_index("batch")
    rows, width = piece.shape
    half = size // 2
    mine = jnp.zeros((half * rows, width), piece.dtype)
    for turn in range(half):
        other = lax.ppermute(piece, "batch", [(at, at ^ (2 * turn)) for at in range(size)]) if turn else piece
        mine = lax.dynamic_update_slice(mine, other, (((me // 2) ^ turn) * rows, 0))
    other = lax.ppermute(mine, "batch", [(at, at ^ 1) for at in range(size)])
    mine, other = mine.reshape(half, rows, width), other.reshape(half, rows, width)
    even = me % 2 == 0
    return jnp.stack([jnp.where(even, mine, other), jnp.where(even, other, mine)], axis=1).reshape(size, rows, width)


def share(rows):
    size = lax.axis_size("batch")
    each = rows.shape[0] // size
    return lax.dynamic_slice(rows, (lax.axis_index("batch") * each, 0), (each, rows.shape[1]))


def norm_parts(values):
    mean = jnp.mean(values, axis=-1, keepdims=True)
    center = values - mean
    spread = jnp.mean(center * center, axis=-1, keepdims=True)
    inverse = lax.rsqrt(spread + EPSILON)
    return center * inverse, inverse


def norm_back(grad, xhat, inverse, gain):
    scaled = grad * gain
    first = jnp.mean(scaled, axis=-1, keepdims=True)
    second = jnp.mean(scaled * xhat, axis=-1, keepdims=True)
    return inverse * (scaled - first - xhat * second)


def gelu_parts(values):
    outer = math.sqrt(2.0 / math.pi)
    inside = jnp.tanh(outer * (values + 0.044715 * values * values * values))
    act = 0.5 * values * (1.0 + inside)
    slope = 0.5 * (1.0 + inside) + 0.5 * values * (1.0 - inside * inside) * outer * (
        1.0 + 3.0 * 0.044715 * values * values
    )
    return act, slope


def mlp_kernel(
    live_ref, hid_ref, mix_ref, out_ref, cot_ref, vec_ref, bup_ref, up_ref, down_ref,
    y_ref, d_s, xhat_s, inv_s, wo_s, gblock_ref, gbup_ref,
    n2_s, y_s, gm_s,
):
    slots = hid_ref.shape[0]
    step = pl.program_id(0)
    live = live_ref[0]

    def live_rows(r0, r1):
        return lax.broadcasted_iota(jnp.int32, (r1 - r0, 1), 0) + r0 < live

    @pl.when(step == 0)
    def _():
        def place(first, rows):
            wo_s[first : first + rows.shape[0], :] = rows

        place_rows(out_ref, 0, out_ref.shape[2], place)
        for r0, r1 in rows_in(slots):
            after = hid_ref[r0:r1, :] + dot_nn(mix_ref[r0:r1, :], wo_s[...]) + vec_ref[0:1, :]
            xhat, inverse = norm_parts(after)
            xhat_s[r0:r1, :] = xhat
            inv_s[r0:r1, :] = inverse
            n2_s[r0:r1, :] = (xhat * vec_ref[1:2, :] + vec_ref[2:3, :]).astype(BF16)
            y_s[r0:r1, :] = after + vec_ref[3:4, :]
            cot = cot_ref[r0:r1, :]
            gm_s[r0:r1, :] = jnp.where(live_rows(r0, r1), cot, jnp.zeros_like(cot))
            d_s[r0:r1, :] = jnp.zeros((r1 - r0, d_s.shape[1]), F32)

    take, count, units, width = up_ref.shape
    up = up_ref[...].reshape(take * count * units, width)
    down = down_ref[...].reshape(take * count * units, width)
    n2 = n2_s[...]
    grad_m = gm_s[...]
    act, slope = gelu_parts(dot_nt(n2, up) + bup_ref[...])
    act = act.astype(BF16)
    grad_u = (dot_nt(grad_m, down) * slope).astype(BF16)
    y_s[...] += dot_nn(act, down)
    d_s[...] += dot_nn(grad_u, up)
    gblock_ref[:, :, 0:units, :] = dot_tn(grad_u, n2).astype(BF16).reshape(take, count, units, width)
    gblock_ref[:, :, units : 2 * units, :] = dot_tn(act, grad_m).astype(BF16).reshape(take, count, units, width)
    gbup_ref[...] = jnp.sum(grad_u.astype(F32), axis=0, keepdims=True)

    @pl.when(step == pl.num_programs(0) - 1)
    def _():
        for r0, r1 in rows_in(slots):
            y_ref[r0:r1, :] = jnp.where(live_rows(r0, r1), y_s[r0:r1, :], 0.0).astype(BF16)


def mlp(live, hidden, mixed, cot, vectors, bias_up, blocks, each):
    slots, width = hidden.shape
    spread, groups = blocks.shape[:2]
    units = 4 * each
    take = TAKE
    steps = spread // take
    chunk = take * groups * units
    one = pl.Buffered(1)

    def whole(shape):
        return pl.BlockSpec(shape, lambda c, live: (0,) * len(shape), pipeline_mode=one)

    full = whole((slots, width))
    flops = 2 * slots * width * (6 * chunk * steps + 3 * width)
    return pl.pallas_call(
        mlp_kernel,
        out_shape=(
            jax.ShapeDtypeStruct((slots, width), BF16),
            jax.ShapeDtypeStruct((slots, width), F32),
            jax.ShapeDtypeStruct((slots, width), F32),
            jax.ShapeDtypeStruct((slots, 1), F32),
            jax.ShapeDtypeStruct((width, width), BF16),
            jax.ShapeDtypeStruct((spread, groups, 2 * units, width), BF16),
            jax.ShapeDtypeStruct((1, steps * chunk), F32),
        ),
        grid_spec=pltpu.PrefetchScalarGridSpec(
            num_scalar_prefetch=1,
            grid=(steps,),
            in_specs=[
                full,
                full,
                pl.BlockSpec((spread, groups, each, width), lambda c, live: (0, 0, 8, 0), pipeline_mode=one),
                full,
                whole((8, width)),
                pl.BlockSpec((1, chunk), lambda c, live: (0, c)),
                pl.BlockSpec((take, groups, units, width), lambda c, live: (c, 0, 0, 0)),
                pl.BlockSpec((take, groups, units, width), lambda c, live: (c, 0, 1, 0)),
            ],
            out_specs=(
                full,
                full,
                full,
                whole((slots, 1)),
                whole((width, width)),
                pl.BlockSpec((take, groups, 2 * units, width), lambda c, live: (c, 0, 0, 0)),
                pl.BlockSpec((1, chunk), lambda c, live: (0, c)),
            ),
            scratch_shapes=[
                pltpu.VMEM((slots, width), BF16),
                pltpu.VMEM((slots, width), F32),
                pltpu.VMEM((slots, width), BF16),
            ],
        ),
        cost_estimate=pl.CostEstimate(
            flops=flops, transcendentals=slots * steps * chunk, bytes_accessed=20 * slots * width + 8 * steps * chunk * width
        ),
        name="mlp",
    )(live, hidden, mixed, blocks, cot, vectors, bias_up, blocks, blocks)


def layer(
    slot_states,
    pass_counts,
    w_qkv,
    q_bias,
    v_bias,
    w_out,
    out_bias,
    w_up,
    up_bias,
    w_down,
    down_bias,
    ln1_gain,
    ln1_bias,
    ln2_gain,
    ln2_bias,
    pass_table,
    cotangent,
):
    groups = lax.axis_size("tensor")
    spread = lax.axis_size("batch")
    me = lax.axis_index("tensor")
    rows, seqs, width = slot_states.shape
    slots = rows * groups
    hidden_here = w_up.shape[1]
    hidden_units = hidden_here * groups
    assert seqs == groups

    gain_one, shift_one = ln1_gain.astype(F32), ln1_bias.astype(F32)
    gain_two, shift_two = ln2_gain.astype(F32), ln2_bias.astype(F32)
    table = pass_table.astype(F32)

    each = width // (groups * spread)
    units = hidden_here // spread
    here = q_bias.shape[0]
    biases = jnp.concatenate([q_bias, v_bias, jnp.zeros((width - 2 * here,), BF16)]).reshape(1, width)
    qkv_rows = w_qkv.transpose(1, 2, 0)
    qkv_piece = jnp.concatenate(
        [share(qkv_rows[part]) for part in range(3)] + [jnp.pad(biases, ((0, 7), (0, 0)))], axis=0
    )
    qkv_blocks = lax.all_gather(gather_tensor(qkv_piece), "batch", axis=0, tiled=False)
    bias_row = jnp.pad(up_bias.reshape(1, width), ((0, 7), (0, 0)))
    mlp_piece = jnp.concatenate([share(w_up.T), share(w_down), share(w_out), bias_row], axis=0)
    mlp_blocks = lax.all_gather(gather_tensor(mlp_piece), "batch", axis=0, tiled=False)
    states = to_sequence(slot_states).astype(F32)

    bias_rows = qkv_blocks[0, :, 3 * each].astype(F32)
    bias_pairs = jnp.stack(
        [bias_rows[:, part * here : (part + 1) * here].reshape(width // LANES, LANES) for part in range(2)], axis=1
    )
    bias_up = mlp_blocks[0, :, 2 * units + each].reshape(groups, spread, units)

    fold = spread if units % 32 == 0 else 8
    if fold != spread:

        def regrouped(values, first, rows):
            rows_of = values[:, :, first : first + rows].transpose(1, 0, 2, 3)
            return rows_of.reshape(groups, fold, -1, width).transpose(1, 0, 2, 3)

        qkv_blocks = jnp.concatenate([regrouped(qkv_blocks, part * each, each) for part in range(3)], axis=2)
        mlp_blocks = jnp.concatenate(
            [
                regrouped(mlp_blocks, 0, units),
                regrouped(mlp_blocks, units, units),
                regrouped(mlp_blocks, 2 * units, each),
            ],
            axis=2,
        )
        bias_up = bias_up.reshape(groups, fold, -1)
    bias_up = bias_up.transpose(1, 0, 2).reshape(1, hidden_units).astype(F32)

    count = lax.dynamic_index_in_dim(pass_counts, me, 0, keepdims=False)
    index = jnp.arange(slots, dtype=jnp.int32)
    passes = (index % count)[:, None]
    live_count = count * LEN
    live_arg = live_count.reshape(1).astype(jnp.int32)
    added = jnp.zeros((slots, width), F32)
    for number in range(PASSES):
        added = jnp.where(passes == number, table[number][None, :], added)
    hidden = states + added

    xhat_one, _ = norm_parts(hidden)
    n1 = (xhat_one * gain_one + shift_one).astype(BF16)
    n1, hidden, passes, cotangent = lax.optimization_barrier((n1, hidden, passes, cotangent))
    fold_each = width // (groups * fold)
    query, keys, values, mixed, lse, matrix = attend(live_arg, n1, qkv_blocks, bias_pairs, fold_each)
    cot, mixed = to_sequence(cotangent, mixed)
    vectors = jnp.stack([out_bias.astype(F32), gain_two, shift_two, down_bias.astype(F32), gain_one])
    vectors = jnp.pad(vectors, ((0, 3), (0, 0)))
    layer_out, grad_n2, xhat_two, inverse_two, matrix_out, mlp_block, grad_bias_up = mlp(
        live_arg, hidden, mixed, cot, vectors, bias_up, mlp_blocks, fold_each
    )
    if fold != spread:
        mlp_block = mlp_block.reshape(fold, groups, 2, -1, width).transpose(1, 2, 0, 3, 4)
        mlp_block = mlp_block.reshape(groups, 2, spread, units, width).transpose(2, 0, 1, 3, 4)
        mlp_block = mlp_block.reshape(spread, groups, 2 * units, width)
    layer_part = to_slots(layer_out)
    extra = 8 if spread * 8 >= 8 + PASSES else 16
    attn_block, grad_h, sums, grad_bias = attend_back(
        live_arg, query, keys, values, mixed, lse, matrix, n1, hidden, passes, grad_n2, xhat_two, inverse_two, cot,
        vectors, matrix_out, fold, groups, extra,
    )
    grad_part = to_slots(grad_h)

    grad_bias_up = grad_bias_up.reshape(fold, groups, -1).transpose(1, 0, 2).reshape(groups, 1, hidden_here)
    lead = 6 + PASSES
    own = jnp.concatenate(
        [
            grad_bias[:, 0, :LANES].reshape(groups, 1, here),
            grad_bias[:, 0, 2 * LANES :].reshape(groups, 1, here),
            jnp.zeros((groups, 1, width - 2 * here), F32),
        ],
        axis=2,
    )
    small = jnp.concatenate(
        [jnp.broadcast_to(sums[None, :lead], (groups, lead, width)), own, grad_bias_up], axis=1
    )
    small = jnp.pad(small, ((0, 0), (0, spread * extra - lead - 2), (0, 0)))
    small = small.reshape(groups, spread, extra, width).transpose(1, 0, 2, 3).astype(BF16)
    if fold != spread:
        attn_block = attn_block[:, :, : 4 * fold_each].reshape(fold, groups, 4, fold_each, width)
        attn_block = attn_block.transpose(1, 2, 0, 3, 4).reshape(groups, 4, spread, each, width)
        attn_block = attn_block.transpose(2, 0, 1, 3, 4).reshape(spread, groups, 4 * each, width)
        attn_block = jnp.pad(attn_block, ((0, 0), (0, 0), (0, extra), (0, 0)))
    attn_block = lax.dynamic_update_slice(attn_block, small, (0, 0, 4 * each, 0))

    def over_tensor(value):
        kept = lax.dynamic_index_in_dim(value, me, 0, keepdims=False).astype(F32)
        for shift in range(1, groups):
            piece = lax.dynamic_index_in_dim(value, (me + shift) % groups, 0, keepdims=False)
            kept = kept + lax.ppermute(piece, "tensor", ring_pairs(groups, shift)).astype(F32)
        return kept.astype(BF16)

    mlp_block = lax.psum_scatter(mlp_block, "batch", scatter_dimension=0, tiled=True)[0]
    attn_block, mlp_block = lax.optimization_barrier((attn_block, mlp_block))
    attn_block = lax.psum_scatter(attn_block, "batch", scatter_dimension=0, tiled=True)[0]
    mlp_piece = over_tensor(mlp_block)
    attn_piece = over_tensor(attn_block)
    mlp_whole = gather_batch(mlp_piece)
    attn_whole = gather_batch(attn_piece)
    parts = [attn_whole[:, part * each : (part + 1) * each].reshape(here, width).astype(F32) for part in range(4)]
    small = attn_whole[:, 4 * each :].reshape(spread * extra, width).astype(F32)
    out_up = mlp_whole[:, :units].reshape(hidden_here, width).astype(F32).T
    out_down = mlp_whole[:, units:].reshape(hidden_here, width).astype(F32)
    out_qkv = jnp.stack(parts[:3], axis=0).transpose(2, 0, 1)
    return (
        layer_part,
        grad_part,
        out_qkv,
        small[lead, :here],
        small[lead, here : 2 * here],
        parts[3],
        small[4],
        out_up,
        small[lead + 1],
        out_down,
        small[5],
        small[0],
        small[1],
        small[2],
        small[3],
        small[6:lead],
    )


def solution(mesh):
    in_specs = (
        P("tensor", "batch", None),
        P("batch"),
        P(None, None, "tensor"),
        P("tensor"),
        P("tensor"),
        P("tensor", None),
        P(),
        P(None, "tensor"),
        P("tensor"),
        P("tensor", None),
        P(),
        P(),
        P(),
        P(),
        P(),
        P(),
        P("tensor", "batch", None),
    )
    out_specs = (
        P("tensor", "batch", None),
        P("tensor", "batch", None),
        P(None, None, "tensor"),
        P("tensor"),
        P("tensor"),
        P("tensor", None),
        P(),
        P(None, "tensor"),
        P("tensor"),
        P("tensor", None),
        P(),
        P(),
        P(),
        P(),
        P(),
        P(),
    )
    return jax.shard_map(layer, mesh=mesh, in_specs=in_specs, out_specs=out_specs, check_vma=False)
```

```python
import functools
import math

import jax
import jax.numpy as jnp
from jax import lax
from jax.experimental import pallas as pl
from jax.experimental.pallas import tpu as pltpu
from jax.sharding import PartitionSpec as P


HEAD_DIM = 64
PASSES = 5
LEN = 192
EPSILON = 1e-05
MASKED = -1e30
QUERY_TILE = 480
TAKE = 2
LANES = 128
F32 = jnp.float32
BF16 = jnp.bfloat16


def tiles_of(slots):
    return [(q0, min(q0 + QUERY_TILE, slots)) for q0 in range(0, slots, QUERY_TILE)]


def rows_in(slots):
    return [(r0, min(r0 + 240, slots)) for r0 in range(0, slots, 240)]


def dot_nt(a, b):
    return lax.dot_general(a, b, (((1,), (1,)), ((), ())), preferred_element_type=F32)


def dot_nn(a, b):
    return lax.dot_general(a, b, (((1,), (0,)), ((), ())), preferred_element_type=F32)


def dot_tn(a, b):
    return lax.dot_general(a, b, (((0,), (0,)), ((), ())), preferred_element_type=F32)


def half_lanes(values, half):
    lane = lax.broadcasted_iota(jnp.int32, (1, LANES), 1)
    return jnp.where((lane // HEAD_DIM) == half, values, jnp.zeros_like(values))


def diagonal_mask(q0, rows, live):
    key = lax.broadcasted_iota(jnp.int32, (rows, rows), 0)
    query = lax.broadcasted_iota(jnp.int32, (rows, rows), 1)
    return (key <= query) & (key + q0 < live)


def place_rows(block_ref, part, each, place):
    spread, groups = block_ref.shape[:2]
    for group in range(groups):
        for member in range(spread):
            rows = block_ref[member, group, part * each : (part + 1) * each, :]
            place((group * spread + member) * each, rows)


def attend_kernel(
    each, live_ref, n1_ref, w_ref, bias_ref, q_ref, k_ref, v_ref, o_ref, lse_ref, matrix_ref, vt_ref
):
    slots = n1_ref.shape[0]
    live = live_ref[0]
    pair = pl.program_id(0)

    @pl.when(pair == 0)
    def _():
        for part in range(3):

            def place(first, rows, part=part):
                done = 0
                while done < rows.shape[0]:
                    at = (first + done) % LANES
                    size = min(rows.shape[0] - done, LANES - at)
                    start = part * LANES + at
                    matrix_ref[(first + done) // LANES, start : start + size, :] = rows[done : done + size, :]
                    done += size

            place_rows(w_ref, part, each, place)

    projected = dot_nt(n1_ref[...], matrix_ref[pair])
    q_ref[...] = (projected[:, :LANES] + bias_ref[0, 0:1, :]).astype(BF16)
    k_ref[...] = projected[:, LANES : 2 * LANES].astype(BF16)
    values = projected[:, 2 * LANES :] + bias_ref[0, 1:2, :]
    v_ref[...] = values.astype(BF16)
    vt_ref[...] = values.T.astype(BF16)
    for q0, q1 in tiles_of(slots):
        rows = q1 - q0

        @pl.when(q0 >= live)
        def _():
            o_ref[q0:q1, :] = jnp.zeros((rows, LANES), BF16)
            lse_ref[0, :, q0:q1] = jnp.zeros((2, rows), F32)

        @pl.when(q0 < live)
        def _():
            query = q_ref[q0:q1, :] * jnp.asarray(1.0 / math.sqrt(HEAD_DIM), BF16)
            allowed = diagonal_mask(q0, rows, live)
            outs = []
            for half in range(2):
                one = half_lanes(query, half)
                last = dot_nt(k_ref[q0:q1, :], one)
                last = jnp.where(allowed, last, MASKED)
                peak = jnp.max(last, axis=0, keepdims=True)
                if q0:
                    early = dot_nt(k_ref[0:q0, :], one)
                    peak = jnp.maximum(peak, jnp.max(early, axis=0, keepdims=True))
                last = jnp.exp(last - peak)
                total = jnp.sum(last, axis=0, keepdims=True)
                lanes = slice(half * HEAD_DIM, (half + 1) * HEAD_DIM)
                if q0:
                    early = jnp.exp(early - peak)
                    total = total + jnp.sum(early, axis=0, keepdims=True)
                out = dot_nn(vt_ref[lanes, q0:q1], last.astype(BF16))
                if q0:
                    out = out + dot_nn(vt_ref[lanes, 0:q0], early.astype(BF16))
                outs.append(out / total)
                lse_ref[0, half : half + 1, q0:q1] = peak + jnp.log(total)
            o_ref[q0:q1, :] = jnp.concatenate(outs, axis=0).T.astype(BF16)


def attend_back_kernel(
    each, live_ref, q_ref, k_ref, v_ref, o_ref, lse_ref, matrix_ref, mixed_ref, n1_ref, hid_ref, pass_ref,
    d_ref, xhat_ref, inv_ref, cot_ref, vec_ref, wo_ref,
    gblock_ref, gh_ref, sums_ref, gbias_ref,
    kt_ref, dk_sum, dv_sum, ga_s, gmix_s, gn1_s, dw_s, gproj_s,
):
    slots = q_ref.shape[0]
    width = n1_ref.shape[1]
    pairs = gmix_s.shape[0]
    spread, groups = gblock_ref.shape[:2]
    live = live_ref[0]
    pair = pl.program_id(0)
    scale = 1.0 / math.sqrt(HEAD_DIM)

    def add_rows(place, value):
        sums_ref[place : place + 1, :] += jnp.sum(value, axis=0, keepdims=True)

    @pl.when(pair == 0)
    def _():
        sums_ref[...] = jnp.zeros_like(sums_ref)
        for r0, r1 in rows_in(slots):
            grad_n2 = d_ref[r0:r1, :]
            xhat = xhat_ref[r0:r1, :]
            alive = lax.broadcasted_iota(jnp.int32, (r1 - r0, 1), 0) + r0 < live
            grad_y = jnp.where(alive, cot_ref[r0:r1, :].astype(F32), 0.0)
            grad_a = grad_y + norm_back(grad_n2, xhat, inv_ref[r0:r1, :], vec_ref[1:2, :])
            ga_s[r0:r1, :] = grad_a
            grad_att = grad_a.astype(BF16)
            gh_ref[r0:r1, :] = grad_att
            grad_mixed = dot_nt(grad_att, wo_ref[...]).astype(BF16)
            for number in range(pairs):
                gmix_s[number, r0:r1, :] = grad_mixed[:, number * LANES : (number + 1) * LANES]
            for place, value in enumerate((grad_n2 * xhat, grad_n2, grad_a, grad_y)):
                add_rows(2 + place, value)
        grad_out = dot_tn(mixed_ref[...], gh_ref[...]).astype(BF16)
        for group in range(groups):
            for member in range(spread):
                first = (group * spread + member) * each
                gblock_ref[member, group, 3 * each : 4 * each, :] = grad_out[first : first + each, :]
                gblock_ref[member, group, 4 * each :, :] = jnp.zeros(
                    (gblock_ref.shape[2] - 4 * each, width), BF16
                )
        gn1_s[...] = jnp.zeros_like(gn1_s)

    kt_ref[...] = k_ref[...].T
    dk_sum[...] = jnp.zeros_like(dk_sum)
    dv_sum[...] = jnp.zeros_like(dv_sum)
    for q0, q1 in tiles_of(slots):
        rows = q1 - q0

        @pl.when(q0 >= live)
        def _():
            gproj_s[q0:q1, :LANES] = jnp.zeros((rows, LANES), BF16)

        @pl.when(q0 < live)
        def _():
            query = q_ref[q0:q1, :] * jnp.asarray(scale, BF16)
            grad = gmix_s[pair, q0:q1, :]
            allowed = diagonal_mask(q0, rows, live)
            both = (grad.astype(F32) * o_ref[q0:q1, :].astype(F32)).T
            parts = []
            for half in range(2):
                lanes = slice(half * HEAD_DIM, (half + 1) * HEAD_DIM)
                one = half_lanes(query, half)
                grad_one = half_lanes(grad, half)
                lse = lse_ref[0, half : half + 1, q0:q1]
                inner = jnp.sum(both[lanes, :], axis=0, keepdims=True)
                turned = None
                for start, stop in ([(0, q0)] if q0 else []) + [(q0, q1)]:
                    scores = dot_nt(k_ref[start:stop, :], one)
                    probs = jnp.exp(scores - lse)
                    if start == q0:
                        probs = jnp.where(allowed, probs, 0.0)
                    grad_weights = dot_nt(v_ref[start:stop, :], grad_one)
                    grad_scores = (probs * (grad_weights - inner)).astype(BF16)
                    dk_sum[start:stop, :] += dot_nn(grad_scores, one)
                    dv_sum[start:stop, :] += dot_nn(probs.astype(BF16), grad_one)
                    piece = dot_nn(kt_ref[lanes, start:stop], grad_scores)
                    turned = piece if turned is None else turned + piece
                parts.append(turned)
            gproj_s[q0:q1, :LANES] = (jnp.concatenate(parts, axis=0).T * scale).astype(BF16)

    gproj_s[:, LANES : 2 * LANES] = dk_sum[...].astype(BF16)
    gproj_s[:, 2 * LANES :] = dv_sum[...].astype(BF16)
    grad_proj = gproj_s[...]
    dw_s[pair] = dot_tn(grad_proj, n1_ref[...]).astype(BF16)
    gn1_s[...] += dot_nn(grad_proj, matrix_ref[0])
    gbias_ref[0] = jnp.sum(grad_proj.astype(F32), axis=0, keepdims=True)

    @pl.when(pair == pairs - 1)
    def _():
        for r0, r1 in rows_in(slots):
            xhat, inverse = norm_parts(hid_ref[r0:r1, :])
            grad_n1 = gn1_s[r0:r1, :]
            grad_h = ga_s[r0:r1, :] + norm_back(grad_n1, xhat, inverse, vec_ref[4:5, :])
            gh_ref[r0:r1, :] = grad_h.astype(BF16)
            add_rows(0, grad_n1 * xhat)
            add_rows(1, grad_n1)
            passes = pass_ref[r0:r1, :]
            for number in range(PASSES):
                add_rows(6 + number, jnp.where(passes == number, grad_h, 0.0))
        for part in range(3):
            for group in range(groups):
                for member in range(spread):
                    first = (group * spread + member) * each
                    done = 0
                    while done < each:
                        at = (first + done) % LANES
                        size = min(each - done, LANES - at)
                        start = part * LANES + at
                        gblock_ref[member, group, part * each + done : part * each + done + size, :] = dw_s[
                            (first + done) // LANES, start : start + size, :
                        ]
                        done += size


def pair_spec(slots):
    return pl.BlockSpec((slots, LANES), lambda p, live: (0, p))


def attend(live, n1, blocks, biases, each):
    slots, width = n1.shape
    pairs = width // LANES
    spec = pair_spec(slots)
    lse_spec = pl.BlockSpec((1, 2, slots), lambda p, live: (p, 0, 0))
    flops = 2 * 2 * slots * slots * width + 2 * slots * width * 3 * width
    shape = jax.ShapeDtypeStruct((slots, width), BF16)
    return pl.pallas_call(
        functools.partial(attend_kernel, each),
        out_shape=(
            shape,
            shape,
            shape,
            shape,
            jax.ShapeDtypeStruct((pairs, 2, slots), F32),
            jax.ShapeDtypeStruct((pairs, 3 * LANES, width), BF16),
        ),
        grid_spec=pltpu.PrefetchScalarGridSpec(
            num_scalar_prefetch=1,
            grid=(pairs,),
            in_specs=[
                pl.BlockSpec((slots, width), lambda p, live: (0, 0), pipeline_mode=pl.Buffered(1)),
                pl.BlockSpec(blocks.shape, lambda p, live: (0, 0, 0, 0), pipeline_mode=pl.Buffered(1)),
                pl.BlockSpec((1, 2, LANES), lambda p, live: (p, 0, 0)),
            ],
            out_specs=(
                spec,
                spec,
                spec,
                spec,
                lse_spec,
                pl.BlockSpec((pairs, 3 * LANES, width), lambda p, live: (0, 0, 0), pipeline_mode=pl.Buffered(1)),
            ),
            scratch_shapes=[pltpu.VMEM((LANES, slots), BF16)],
        ),
        cost_estimate=pl.CostEstimate(
            flops=flops, transcendentals=slots * slots * width // HEAD_DIM, bytes_accessed=16 * slots * width
        ),
        name="attend",
    )(live, n1, blocks, biases)


def attend_back(
    live, query, keys, values, mixed, lse, matrix, n1, hidden, passes, grad_n2, xhat, inverse, cot, vectors, w_out,
    spread, groups, extra,
):
    slots, width = query.shape
    pairs = width // LANES
    each = width // (spread * groups)
    one = pl.Buffered(1)
    spec = pair_spec(slots)

    def whole(shape):
        return pl.BlockSpec(shape, lambda p, live: (0,) * len(shape), pipeline_mode=one)

    full = whole((slots, width))
    column = whole((slots, 1))
    flops = 5 * 2 * slots * slots * width + 2 * slots * width * 8 * width
    return pl.pallas_call(
        functools.partial(attend_back_kernel, each),
        out_shape=(
            jax.ShapeDtypeStruct((spread, groups, 4 * each + extra, width), BF16),
            jax.ShapeDtypeStruct((slots, width), BF16),
            jax.ShapeDtypeStruct((16, width), F32),
            jax.ShapeDtypeStruct((pairs, 1, 3 * LANES), F32),
        ),
        grid_spec=pltpu.PrefetchScalarGridSpec(
            num_scalar_prefetch=1,
            grid=(pairs,),
            in_specs=[
                spec,
                spec,
                spec,
                spec,
                pl.BlockSpec((1, 2, slots), lambda p, live: (p, 0, 0)),
                pl.BlockSpec((1, 3 * LANES, width), lambda p, live: (p, 0, 0)),
                full,
                full,
                full,
                column,
                full,
                full,
                column,
                full,
                whole((8, width)),
                whole((width, width)),
            ],
            out_specs=(
                whole((spread, groups, 4 * each + extra, width)),
                full,
                whole((16, width)),
                pl.BlockSpec((1, 1, 3 * LANES), lambda p, live: (p, 0, 0)),
            ),
            scratch_shapes=[
                pltpu.VMEM((LANES, slots), BF16),
                pltpu.VMEM((slots, LANES), F32),
                pltpu.VMEM((slots, LANES), F32),
                pltpu.VMEM((slots, width), F32),
                pltpu.VMEM((pairs, slots, LANES), BF16),
                pltpu.VMEM((slots, width), F32),
                pltpu.VMEM((pairs, 3 * LANES, width), BF16),
                pltpu.VMEM((slots, 3 * LANES), BF16),
            ],
        ),
        cost_estimate=pl.CostEstimate(
            flops=flops, transcendentals=slots * slots * width // HEAD_DIM, bytes_accessed=40 * slots * width
        ),
        name="attend_back",
    )(
        live, query, keys, values, mixed, lse, matrix, mixed, n1, hidden, passes, grad_n2, xhat, inverse, cot,
        vectors, w_out,
    )


def ring_pairs(size, shift):
    return [(source, (source + shift) % size) for source in range(size)]


def to_sequence(block, hold=None):
    size = lax.axis_size("tensor")
    me = lax.axis_index("tensor")
    rows, _, width = block.shape
    block = lax.optimization_barrier(block.transpose(1, 0, 2))
    pieces = []
    for shift in range(size):
        piece = lax.dynamic_index_in_dim(block, (me + shift) % size, 0, keepdims=False)
        pieces.append(lax.ppermute(piece, "tensor", ring_pairs(size, shift)) if shift else piece)
    if hold is not None:
        pieces, hold = lax.optimization_barrier((pieces, hold))
    out = jnp.zeros((size * rows, width), block.dtype)
    for shift, piece in enumerate(pieces):
        out = lax.dynamic_update_slice(out, piece, (((me - shift) % size) * rows, 0))
    return (out, hold) if hold is not None else out


def send_slots(values):
    size = lax.axis_size("tensor")
    me = lax.axis_index("tensor")
    slots, width = values.shape
    rows = slots // size
    pieces = []
    for shift in range(size):
        piece = lax.dynamic_slice(values, (((me + shift) % size) * rows, 0), (rows, width))
        pieces.append(lax.ppermute(piece, "tensor", ring_pairs(size, shift)) if shift else piece)
    return pieces


def join_slots(pieces, hold=None):
    size = len(pieces)
    me = lax.axis_index("tensor")
    rows, width = pieces[0].shape
    if hold is not None:
        pieces, _ = lax.optimization_barrier((pieces, hold))
    out = jnp.zeros((size * rows, width), pieces[0].dtype)
    for shift, piece in enumerate(pieces):
        out = lax.dynamic_update_slice(out, piece, (((me - shift) % size) * rows, 0))
    return lax.optimization_barrier(out).reshape(size, rows, width).transpose(1, 0, 2)


def gather_tensor(piece):
    size = lax.axis_size("tensor")
    me = lax.axis_index("tensor")
    rows, width = piece.shape
    out = jnp.zeros((size * rows, width), piece.dtype)
    for shift in range(size):
        other = lax.ppermute(piece, "tensor", ring_pairs(size, shift)) if shift else piece
        out = lax.dynamic_update_slice(out, other, (((me - shift) % size) * rows, 0))
    return out.reshape(size, rows, width)


def gather_batch(piece):
    size = lax.axis_size("batch")
    if size != 8:
        return lax.all_gather(piece, "batch", axis=0, tiled=False)
    me = lax.axis_index("batch")
    rows, width = piece.shape
    half = size // 2
    mine = jnp.zeros((half * rows, width), piece.dtype)
    for turn in range(half):
        other = lax.ppermute(piece, "batch", [(at, at ^ (2 * turn)) for at in range(size)]) if turn else piece
        mine = lax.dynamic_update_slice(mine, other, (((me // 2) ^ turn) * rows, 0))
    other = lax.ppermute(mine, "batch", [(at, at ^ 1) for at in range(size)])
    mine, other = mine.reshape(half, rows, width), other.reshape(half, rows, width)
    even = me % 2 == 0
    return jnp.stack([jnp.where(even, mine, other), jnp.where(even, other, mine)], axis=1).reshape(size, rows, width)


def share(rows):
    size = lax.axis_size("batch")
    each = rows.shape[0] // size
    return lax.dynamic_slice(rows, (lax.axis_index("batch") * each, 0), (each, rows.shape[1]))


def norm_parts(values):
    mean = jnp.mean(values, axis=-1, keepdims=True)
    center = values - mean
    spread = jnp.mean(center * center, axis=-1, keepdims=True)
    inverse = lax.rsqrt(spread + EPSILON)
    return center * inverse, inverse


def norm_back(grad, xhat, inverse, gain):
    scaled = grad * gain
    first = jnp.mean(scaled, axis=-1, keepdims=True)
    second = jnp.mean(scaled * xhat, axis=-1, keepdims=True)
    return inverse * (scaled - first - xhat * second)


def gelu_parts(values):
    outer = math.sqrt(2.0 / math.pi)
    inside = jnp.tanh(outer * (values + 0.044715 * values * values * values))
    act = 0.5 * values * (1.0 + inside)
    slope = 0.5 * (1.0 + inside) + 0.5 * values * (1.0 - inside * inside) * outer * (
        1.0 + 3.0 * 0.044715 * values * values
    )
    return act, slope


def mlp_kernel(
    live_ref, hid_ref, mix_ref, out_ref, cot_ref, vec_ref, bup_ref, up_ref, down_ref,
    y_ref, d_s, xhat_s, inv_s, wo_s, gblock_ref, gbup_ref,
    n2_s, y_s, gm_s,
):
    slots = hid_ref.shape[0]
    step = pl.program_id(0)
    live = live_ref[0]

    def live_rows(r0, r1):
        return lax.broadcasted_iota(jnp.int32, (r1 - r0, 1), 0) + r0 < live

    @pl.when(step == 0)
    def _():
        def place(first, rows):
            wo_s[first : first + rows.shape[0], :] = rows

        place_rows(out_ref, 0, out_ref.shape[2], place)
        for r0, r1 in rows_in(slots):
            after = hid_ref[r0:r1, :] + dot_nn(mix_ref[r0:r1, :], wo_s[...]) + vec_ref[0:1, :]
            xhat, inverse = norm_parts(after)
            xhat_s[r0:r1, :] = xhat
            inv_s[r0:r1, :] = inverse
            n2_s[r0:r1, :] = (xhat * vec_ref[1:2, :] + vec_ref[2:3, :]).astype(BF16)
            y_s[r0:r1, :] = after + vec_ref[3:4, :]
            cot = cot_ref[r0:r1, :]
            gm_s[r0:r1, :] = jnp.where(live_rows(r0, r1), cot, jnp.zeros_like(cot))
            d_s[r0:r1, :] = jnp.zeros((r1 - r0, d_s.shape[1]), F32)

    take, count, units, width = up_ref.shape
    up = up_ref[...].reshape(take * count * units, width)
    down = down_ref[...].reshape(take * count * units, width)
    n2 = n2_s[...]
    grad_m = gm_s[...]
    act, slope = gelu_parts(dot_nt(n2, up) + bup_ref[...])
    act = act.astype(BF16)
    grad_u = (dot_nt(grad_m, down) * slope).astype(BF16)
    y_s[...] += dot_nn(act, down)
    d_s[...] += dot_nn(grad_u, up)
    gblock_ref[:, :, 0:units, :] = dot_tn(grad_u, n2).astype(BF16).reshape(take, count, units, width)
    gblock_ref[:, :, units : 2 * units, :] = dot_tn(act, grad_m).astype(BF16).reshape(take, count, units, width)
    gbup_ref[...] = jnp.sum(grad_u.astype(F32), axis=0, keepdims=True)

    @pl.when(step == pl.num_programs(0) - 1)
    def _():
        for r0, r1 in rows_in(slots):
            y_ref[r0:r1, :] = jnp.where(live_rows(r0, r1), y_s[r0:r1, :], 0.0).astype(BF16)


def mlp(live, hidden, mixed, cot, vectors, bias_up, blocks, each):
    slots, width = hidden.shape
    spread, groups = blocks.shape[:2]
    units = 4 * each
    take = TAKE
    steps = spread // take
    chunk = take * groups * units
    one = pl.Buffered(1)

    def whole(shape):
        return pl.BlockSpec(shape, lambda c, live: (0,) * len(shape), pipeline_mode=one)

    full = whole((slots, width))
    flops = 2 * slots * width * (6 * chunk * steps + 3 * width)
    return pl.pallas_call(
        mlp_kernel,
        out_shape=(
            jax.ShapeDtypeStruct((slots, width), BF16),
            jax.ShapeDtypeStruct((slots, width), F32),
            jax.ShapeDtypeStruct((slots, width), F32),
            jax.ShapeDtypeStruct((slots, 1), F32),
            jax.ShapeDtypeStruct((width, width), BF16),
            jax.ShapeDtypeStruct((spread, groups, 2 * units, width), BF16),
            jax.ShapeDtypeStruct((1, steps * chunk), F32),
        ),
        grid_spec=pltpu.PrefetchScalarGridSpec(
            num_scalar_prefetch=1,
            grid=(steps,),
            in_specs=[
                full,
                full,
                pl.BlockSpec((spread, groups, each, width), lambda c, live: (0, 0, 8, 0), pipeline_mode=one),
                full,
                whole((8, width)),
                pl.BlockSpec((1, chunk), lambda c, live: (0, c)),
                pl.BlockSpec((take, groups, units, width), lambda c, live: (c, 0, 0, 0)),
                pl.BlockSpec((take, groups, units, width), lambda c, live: (c, 0, 1, 0)),
            ],
            out_specs=(
                full,
                full,
                full,
                whole((slots, 1)),
                whole((width, width)),
                pl.BlockSpec((take, groups, 2 * units, width), lambda c, live: (c, 0, 0, 0)),
                pl.BlockSpec((1, chunk), lambda c, live: (0, c)),
            ),
            scratch_shapes=[
                pltpu.VMEM((slots, width), BF16),
                pltpu.VMEM((slots, width), F32),
                pltpu.VMEM((slots, width), BF16),
            ],
        ),
        cost_estimate=pl.CostEstimate(
            flops=flops, transcendentals=slots * steps * chunk, bytes_accessed=20 * slots * width + 8 * steps * chunk * width
        ),
        name="mlp",
    )(live, hidden, mixed, blocks, cot, vectors, bias_up, blocks, blocks)


def layer(
    slot_states,
    pass_counts,
    w_qkv,
    q_bias,
    v_bias,
    w_out,
    out_bias,
    w_up,
    up_bias,
    w_down,
    down_bias,
    ln1_gain,
    ln1_bias,
    ln2_gain,
    ln2_bias,
    pass_table,
    cotangent,
):
    groups = lax.axis_size("tensor")
    spread = lax.axis_size("batch")
    me = lax.axis_index("tensor")
    rows, seqs, width = slot_states.shape
    slots = rows * groups
    hidden_here = w_up.shape[1]
    hidden_units = hidden_here * groups
    assert seqs == groups

    gain_one, shift_one = ln1_gain.astype(F32), ln1_bias.astype(F32)
    gain_two, shift_two = ln2_gain.astype(F32), ln2_bias.astype(F32)
    table = pass_table.astype(F32)

    each = width // (groups * spread)
    units = hidden_here // spread
    here = q_bias.shape[0]
    biases = jnp.concatenate([q_bias, v_bias, jnp.zeros((width - 2 * here,), BF16)]).reshape(1, width)
    qkv_rows = w_qkv.transpose(1, 2, 0)
    qkv_piece = jnp.concatenate(
        [share(qkv_rows[part]) for part in range(3)] + [jnp.pad(biases, ((0, 7), (0, 0)))], axis=0
    )
    qkv_blocks = lax.all_gather(gather_tensor(qkv_piece), "batch", axis=0, tiled=False)
    bias_row = jnp.pad(up_bias.reshape(1, width), ((0, 7), (0, 0)))
    mlp_piece = jnp.concatenate([share(w_up.T), share(w_down), share(w_out), bias_row], axis=0)
    mlp_blocks = lax.all_gather(gather_tensor(mlp_piece), "batch", axis=0, tiled=False)
    states = to_sequence(slot_states).astype(F32)

    bias_rows = qkv_blocks[0, :, 3 * each].astype(F32)
    bias_pairs = jnp.stack(
        [bias_rows[:, part * here : (part + 1) * here].reshape(width // LANES, LANES) for part in range(2)], axis=1
    )
    bias_up = mlp_blocks[0, :, 2 * units + each].reshape(groups, spread, units)

    fold = spread if units % 32 == 0 else 8
    if fold != spread:

        def regrouped(values, first, rows):
            rows_of = values[:, :, first : first + rows].transpose(1, 0, 2, 3)
            return rows_of.reshape(groups, fold, -1, width).transpose(1, 0, 2, 3)

        qkv_blocks = jnp.concatenate([regrouped(qkv_blocks, part * each, each) for part in range(3)], axis=2)
        mlp_blocks = jnp.concatenate(
            [
                regrouped(mlp_blocks, 0, units),
                regrouped(mlp_blocks, units, units),
                regrouped(mlp_blocks, 2 * units, each),
            ],
            axis=2,
        )
        bias_up = bias_up.reshape(groups, fold, -1)
    bias_up = bias_up.transpose(1, 0, 2).reshape(1, hidden_units).astype(F32)

    count = lax.dynamic_index_in_dim(pass_counts, me, 0, keepdims=False)
    index = jnp.arange(slots, dtype=jnp.int32)
    passes = (index % count)[:, None]
    live_count = count * LEN
    live_arg = live_count.reshape(1).astype(jnp.int32)
    added = jnp.zeros((slots, width), F32)
    for number in range(PASSES):
        added = jnp.where(passes == number, table[number][None, :], added)
    hidden = states + added

    xhat_one, _ = norm_parts(hidden)
    n1 = (xhat_one * gain_one + shift_one).astype(BF16)
    n1, hidden, passes, cotangent = lax.optimization_barrier((n1, hidden, passes, cotangent))
    fold_each = width // (groups * fold)
    query, keys, values, mixed, lse, matrix = attend(live_arg, n1, qkv_blocks, bias_pairs, fold_each)
    cot, mixed = to_sequence(cotangent, mixed)
    vectors = jnp.stack([out_bias.astype(F32), gain_two, shift_two, down_bias.astype(F32), gain_one])
    vectors = jnp.pad(vectors, ((0, 3), (0, 0)))
    layer_out, grad_n2, xhat_two, inverse_two, matrix_out, mlp_block, grad_bias_up = mlp(
        live_arg, hidden, mixed, cot, vectors, bias_up, mlp_blocks, fold_each
    )
    if fold != spread:
        mlp_block = mlp_block.reshape(fold, groups, 2, -1, width).transpose(1, 2, 0, 3, 4)
        mlp_block = mlp_block.reshape(groups, 2, spread, units, width).transpose(2, 0, 1, 3, 4)
        mlp_block = mlp_block.reshape(spread, groups, 2 * units, width)
    layer_pieces = send_slots(layer_out)
    extra = 8 if spread * 8 >= 8 + PASSES else 16
    attn_block, grad_h, sums, grad_bias = attend_back(
        live_arg, query, keys, values, mixed, lse, matrix, n1, hidden, passes, grad_n2, xhat_two, inverse_two, cot,
        vectors, matrix_out, fold, groups, extra,
    )
    grad_pieces = send_slots(grad_h)

    grad_bias_up = grad_bias_up.reshape(fold, groups, -1).transpose(1, 0, 2).reshape(groups, 1, hidden_here)
    lead = 6 + PASSES
    own = jnp.concatenate(
        [
            grad_bias[:, 0, :LANES].reshape(groups, 1, here),
            grad_bias[:, 0, 2 * LANES :].reshape(groups, 1, here),
            jnp.zeros((groups, 1, width - 2 * here), F32),
        ],
        axis=2,
    )
    small = jnp.concatenate(
        [jnp.broadcast_to(sums[None, :lead], (groups, lead, width)), own, grad_bias_up], axis=1
    )
    small = jnp.pad(small, ((0, 0), (0, spread * extra - lead - 2), (0, 0)))
    small = small.reshape(groups, spread, extra, width).transpose(1, 0, 2, 3).astype(BF16)
    if fold != spread:
        attn_block = attn_block[:, :, : 4 * fold_each].reshape(fold, groups, 4, fold_each, width)
        attn_block = attn_block.transpose(1, 2, 0, 3, 4).reshape(groups, 4, spread, each, width)
        attn_block = attn_block.transpose(2, 0, 1, 3, 4).reshape(spread, groups, 4 * each, width)
        attn_block = jnp.pad(attn_block, ((0, 0), (0, 0), (0, extra), (0, 0)))
    attn_block = lax.dynamic_update_slice(attn_block, small, (0, 0, 4 * each, 0))

    def over_tensor(value):
        kept = lax.dynamic_index_in_dim(value, me, 0, keepdims=False).astype(F32)
        for shift in range(1, groups):
            piece = lax.dynamic_index_in_dim(value, (me + shift) % groups, 0, keepdims=False)
            kept = kept + lax.ppermute(piece, "tensor", ring_pairs(groups, shift)).astype(F32)
        return kept.astype(BF16)

    mlp_block = lax.psum_scatter(mlp_block, "batch", scatter_dimension=0, tiled=True)[0]
    attn_block, mlp_block = lax.optimization_barrier((attn_block, mlp_block))
    attn_block = lax.psum_scatter(attn_block, "batch", scatter_dimension=0, tiled=True)[0]
    mlp_piece = over_tensor(mlp_block)
    attn_piece = over_tensor(attn_block)
    layer_part = join_slots(layer_pieces)
    grad_part = join_slots(grad_pieces)
    mlp_whole = gather_batch(mlp_piece)
    attn_whole = gather_batch(attn_piece)
    parts = [attn_whole[:, part * each : (part + 1) * each].reshape(here, width).astype(F32) for part in range(4)]
    small = attn_whole[:, 4 * each :].reshape(spread * extra, width).astype(F32)
    out_up = mlp_whole[:, :units].reshape(hidden_here, width).astype(F32).T
    out_down = mlp_whole[:, units:].reshape(hidden_here, width).astype(F32)
    out_qkv = jnp.stack(parts[:3], axis=0).transpose(2, 0, 1)
    return (
        layer_part,
        grad_part,
        out_qkv,
        small[lead, :here],
        small[lead, here : 2 * here],
        parts[3],
        small[4],
        out_up,
        small[lead + 1],
        out_down,
        small[5],
        small[0],
        small[1],
        small[2],
        small[3],
        small[6:lead],
    )


def solution(mesh):
    in_specs = (
        P("tensor", "batch", None),
        P("batch"),
        P(None, None, "tensor"),
        P("tensor"),
        P("tensor"),
        P("tensor", None),
        P(),
        P(None, "tensor"),
        P("tensor"),
        P("tensor", None),
        P(),
        P(),
        P(),
        P(),
        P(),
        P(),
        P("tensor", "batch", None),
    )
    out_specs = (
        P("tensor", "batch", None),
        P("tensor", "batch", None),
        P(None, None, "tensor"),
        P("tensor"),
        P("tensor"),
        P("tensor", None),
        P(),
        P(None, "tensor"),
        P("tensor"),
        P("tensor", None),
        P(),
        P(),
        P(),
        P(),
        P(),
        P(),
    )
    return jax.shard_map(layer, mesh=mesh, in_specs=in_specs, out_specs=out_specs, check_vma=False)
```
